32 devices in a mesh: dom: 4 (over y, x), head: 8 (over z, core).
Axes of the slice: x: 2, y: 2, z: 4, core: 2. Of those that a mesh axis runs over, the one named last changes fastest.
Arguments:
- node_queries: bfloat16 [8192, 1024], P(('dom', 'head')), may hold values from -20 to 20
- node_keys: bfloat16 [8192, 1024], P(('dom', 'head')), may hold values from -20 to 20
- node_values: bfloat16 [8192, 1024], P(('dom', 'head')), may hold values from -6 to 6
- out_grad: bfloat16 [8192, 1024], P(('dom', 'head')), may hold values from -6 to 6
- degrees: int32 [8192], P('dom'), may hold values from 8 to 4096
- neighbor_blocks: int32 [64, 12], P('dom'), may hold values from 0 to 31, as said below
- send_slots: int32 [4, 4, 4], replicated, may hold values from -1 to 15, as said below
Outputs:
- grad_queries: bfloat16 [8192, 1024], P(('dom', 'head'))
- grad_keys: bfloat16 [8192, 1024], P(('dom', 'head'))
- grad_values: bfloat16 [8192, 1024], P(('dom', 'head'))
The draws below stay inside these ranges and needn't reach their ends.
Inputs may be any that keep to these rules, and one draw needn't show every extreme that they name: `neighbor_blocks`: an entry t below 16 names block t of the row's own partition; entry 16 + q * 4 + s names slot s of send_slots[q, p] for the row's partition p, and that slot is live. The 12 entries of a row are distinct, and every live slot listed for a partition is named by some row block of it. send_slots[q, p] holds distinct local block numbers of partition q, live slots first and -1 in empty ones; send_slots[p, p] is empty; for every destination p at least one source fills all 4 slots, every other source fills 1 to 4.
All inputs are finite; a program needn't handle non-finite values.
Results may differ from the reference program's by a relative error of at most 0.0068.
Values may be sent and summed in bfloat16 or wider, within the bound.
No kernel may reach another device: no remote copies, remote signals or barrier semaphores. Data moves between devices by JAX's collectives and lax.ppermute only.
A program may use at most 128 MiB of HBM per device.

```python
import math
import jax
import jax.numpy as jnp
from jax import lax

D = 1024
H = 16
NBR = 12
BS = 128
CAP = 4
BLK_DOM = 16
TOTAL_BLK = 64
NODES = 8192
SLOTS = 32
N_DOM = 4


def plan_tables(key):
    parts = N_DOM
    nblk = BLK_DOM
    key_count, key_shift, key_order, key_local, key_remote = jax.random.split(jax.random.fold_in(key, 101), 5)
    counts = jax.random.randint(key_count, (parts, parts), 1, CAP + 1)
    shift = jax.random.randint(key_shift, (), 1, parts)
    source = jnp.arange(parts)[:, None]
    target = jnp.arange(parts)[None, :]
    counts = jnp.where(target == (source + shift) % parts, CAP, counts)
    counts = jnp.where(target == source, 0, counts)
    scores = jax.random.randint(key_order, (parts, parts, nblk), 0, 1 << 20) * nblk + jnp.arange(nblk)
    order = jnp.argsort(scores, axis=-1)[:, :, :CAP]
    live = jnp.arange(CAP)[None, None, :] < counts[:, :, None]
    send = jnp.where(live, order, -1).astype(jnp.int32)
    others_scores = jax.random.randint(key_local, (parts * nblk, nblk - 1), 0, 1 << 20) * (nblk - 1) + jnp.arange(nblk - 1)
    others_pick = jnp.argsort(others_scores, axis=-1)[:, :NBR - 4]
    own = jnp.tile(jnp.arange(nblk), parts)
    others = (own[:, None] + 1 + others_pick) % nblk
    valid = jnp.transpose(live, (1, 0, 2)).reshape(parts, parts * CAP)
    flat = jnp.arange(parts * CAP)
    remote_scores = jnp.where(valid, jax.random.randint(key_remote, (parts, parts * CAP), 0, 1 << 20) * (parts * CAP) + flat, (1 << 30) + flat)
    remote_order = jnp.argsort(remote_scores, axis=-1)
    live_count = jnp.sum(valid.astype(jnp.int32), axis=-1)
    where_at = (3 * jnp.arange(nblk)[None, :, None] + jnp.arange(3)[None, None, :]) % live_count[:, None, None]
    chosen = jnp.take_along_axis(remote_order, where_at.reshape(parts, -1), axis=1).reshape(parts * nblk, 3)
    rows = jnp.concatenate([own[:, None], others, nblk + chosen], axis=1).astype(jnp.int32)
    return (rows, send)


def draw_neighbor_blocks(key, part):
    return plan_tables(key)[0]


def draw_send_slots(key, part):
    return plan_tables(key)[1]


def attention_inputs(key):
    key_q, key_k = jax.random.split(jax.random.fold_in(key, 202), 2)
    shape = (NODES, D)
    queries = jax.random.truncated_normal(key_q, -4.0, 4.0, shape)
    keys_out = jax.random.truncated_normal(key_k, -4.0, 4.0, shape)
    return (queries.astype(jnp.bfloat16), keys_out.astype(jnp.bfloat16))


def draw_node_queries(key, part):
    return attention_inputs(key)[0]


def draw_node_keys(key, part):
    return attention_inputs(key)[1]


def plant(entries, rng, low, high):
    longest = entries.shape.index(max(entries.shape))
    spots = []
    for shift in (0, 1):
        where = [jax.random.randint(jax.random.fold_in(rng, axis), (), 0, length) for axis, length in enumerate(entries.shape)]
        where[longest] = (where[longest] + shift) % entries.shape[longest]
        spots.append(tuple(where))
    return entries.at[spots[0]].set(low).at[spots[1]].set(high)


def level_of(stream_key, shape, cuts, smallest, largest):
    factor_of, own = 1.0, jax.random.fold_in(stream_key, 6)
    for axis_at, shards_of in cuts:
        steps = jnp.exp(jax.random.uniform(jax.random.fold_in(own, axis_at), (shards_of,), jnp.float32, smallest / len(cuts), largest / len(cuts)))
        factor_of = factor_of * jnp.repeat(steps, shape[axis_at] // shards_of).reshape([-1 if axis == axis_at else 1 for axis in range(len(shape))])
    return factor_of


def noise(key, shape, width, most, cuts=(), kind=jnp.bfloat16):
    loudness = level_of(key, shape, cuts, -0.22, 0.18) if cuts else 1.0
    result = jax.random.normal(key, shape, jnp.float32) * width * loudness
    return jnp.minimum(jnp.maximum(result, -most), most).astype(kind)


def setup_inputs(seed: int = 0) -> dict:
    seeds = jax.random.split(jax.random.key(seed), 8)
    node_queries = draw_node_queries(jax.random.fold_in(seeds[7], 71), 0)
    node_keys = draw_node_keys(jax.random.fold_in(seeds[7], 71), 0)
    node_values = noise(seeds[2], (NODES, D), 1.0, 6.0, ((0, 32),))
    out_grad = noise(seeds[3], (NODES, D), 1.0, 6.0, ((0, 32),))
    degrees = plant(jax.random.randint(seeds[4], (NODES,), 8, 4097), jax.random.fold_in(seeds[4], 1), 8, 4096).astype(jnp.int32)
    neighbor_blocks = draw_neighbor_blocks(jax.random.fold_in(seeds[7], 71), 0)
    send_slots = draw_send_slots(jax.random.fold_in(seeds[7], 71), 0)
    return {"node_queries": node_queries, "node_keys": node_keys, "node_values": node_values, "out_grad": out_grad, "degrees": degrees, "neighbor_blocks": neighbor_blocks, "send_slots": send_slots}


def reference(node_queries, node_keys, node_values, out_grad, degrees, neighbor_blocks, send_slots):
    head_dim = D // H
    nblk = BLK_DOM
    kv_blocks = jnp.stack([node_keys, node_values], 1).reshape(TOTAL_BLK, BS, 2, H, head_dim)
    q_blocks = node_queries.reshape(TOTAL_BLK, BS, H, head_dim)
    g_blocks = out_grad.reshape(TOTAL_BLK, BS, H, head_dim)
    scale_all = (jnp.log(degrees.astype(jnp.float32)) / math.log(64.0) / math.sqrt(head_dim)).reshape(TOTAL_BLK, BS)
    clamped = jnp.maximum(send_slots, 0).astype(jnp.int32)

    def one_part(carry, part):
        local_ids = part * nblk + jnp.arange(nblk, dtype=jnp.int32)
        remote_ids = (jnp.arange(N_DOM, dtype=jnp.int32)[:, None] * nblk + clamped[:, part, :]).reshape(-1)
        slot_ids = jnp.concatenate([local_ids, remote_ids]).astype(jnp.int32)
        table = kv_blocks[slot_ids]

        def group(acc, index):
            rows = (part * nblk + index * 4 + jnp.arange(4, dtype=jnp.int32)).astype(jnp.int32)
            picks = neighbor_blocks[rows]
            gathered = table[picks.reshape(-1)].reshape(4, NBR * BS, 2, H, head_dim).astype(jnp.float32)
            keys_n = gathered[:, :, 0]
            values_n = gathered[:, :, 1]
            queries_g = q_blocks[rows].astype(jnp.float32)
            grads_g = g_blocks[rows].astype(jnp.float32)
            scale = scale_all[rows][:, None, :, None]
            scores = jnp.einsum('gihd,gjhd->ghij', queries_g, keys_n) * scale
            top = lax.optimization_barrier(jnp.max(scores, axis=-1, keepdims=True))
            expo = jnp.exp(scores - top)
            probs = expo / lax.optimization_barrier(jnp.sum(expo, axis=-1, keepdims=True))
            dprobs = jnp.einsum('gihd,gjhd->ghij', grads_g, values_n)
            delta = lax.optimization_barrier(jnp.sum(probs * dprobs, axis=-1, keepdims=True))
            dscores = lax.optimization_barrier((probs * (dprobs - delta) * scale).astype(jnp.bfloat16)).astype(jnp.float32)
            probs_b = lax.optimization_barrier(probs.astype(jnp.bfloat16)).astype(jnp.float32)
            dq = jnp.einsum('ghij,gjhd->gihd', dscores, keys_n)
            dk = jnp.einsum('ghij,gihd->gjhd', dscores, queries_g)
            dv = jnp.einsum('ghij,gihd->gjhd', probs_b, grads_g)
            contrib = jnp.stack([dk, dv], 2).reshape(4 * NBR, BS, 2, H, head_dim)
            acc = acc.at[picks.reshape(-1)].add(contrib)
            return (acc, dq.astype(jnp.bfloat16))
        acc0 = jnp.zeros((SLOTS, BS, 2, H, head_dim), jnp.float32)
        acc, dq = lax.scan(group, acc0, jnp.arange(nblk // 4, dtype=jnp.int32))
        carry = carry.at[local_ids].add(acc[:nblk])
        remote = acc[nblk:].astype(jnp.bfloat16).astype(jnp.float32)
        carry = carry.at[remote_ids].add(remote)
        return (carry, dq.reshape(nblk, BS, H, head_dim))
    total0 = jnp.zeros((TOTAL_BLK, BS, 2, H, head_dim), jnp.float32)
    total, dq_all = lax.scan(one_part, total0, jnp.arange(N_DOM, dtype=jnp.int32))
    grads = total.astype(jnp.bfloat16)
    grad_queries = dq_all.reshape(NODES, D)
    grad_keys = grads[:, :, 0].reshape(NODES, D)
    grad_values = grads[:, :, 1].reshape(NODES, D)
    return (grad_queries, grad_keys, grad_values)
```

```python
import functools
import math

import jax
import jax.numpy as jnp
from jax import lax
from jax.experimental import pallas as pl
from jax.experimental.pallas import tpu as pltpu
from jax.sharding import PartitionSpec as P

D = 1024
H = 16
NBR = 12
BS = 128
HD = D // H
LOG2E = 1.4426950408889634
VMEM_LIMIT = 56 << 20

bf16 = jnp.bfloat16
f32 = jnp.float32


def params():
    return pltpu.CompilerParams(vmem_limit_bytes=VMEM_LIMIT)


def cost(flops, bytes_accessed):
    return pl.CostEstimate(flops=flops, bytes_accessed=bytes_accessed, transcendentals=0)


VMEM = pl.BlockSpec(memory_space=pltpu.VMEM)
SMEM = pl.BlockSpec(memory_space=pltpu.SMEM)
ANY = pl.BlockSpec(memory_space=pl.ANY)


def pack_kernel(first, n, q_ref, k_ref, v_ref, g_ref, out_ref):
    rows = q_ref.shape[0]
    for j in range(n):
        cols = pl.ds((first + j) * HD, HD)
        out_ref[j, pl.ds(0, rows), pl.ds(0, HD)] = k_ref[:, cols]
        out_ref[j, pl.ds(0, rows), pl.ds(HD, HD)] = v_ref[:, cols]
        out_ref[j, pl.ds(rows, rows), pl.ds(0, HD)] = q_ref[:, cols]
        out_ref[j, pl.ds(rows, rows), pl.ds(HD, HD)] = g_ref[:, cols]


def pack(queries, keys, values, grads, phase, n):
    rows = queries.shape[0]
    return pl.pallas_call(
        functools.partial(pack_kernel, phase * n, n),
        out_shape=jax.ShapeDtypeStruct((n, 2 * rows, 2 * HD), bf16),
        in_specs=[VMEM] * 4,
        out_specs=VMEM,
        compiler_params=params(),
        cost_estimate=cost(0, 12 * rows * D),
        name="pack",
    )(queries, keys, values, grads)


def lend_kernel(parts, cap, bpd, lists_ref, kv_ref, *outs):
    for k in range(1, parts):
        for s in range(cap):
            b = lists_ref[k * cap + s]
            outs[k - 1][s] = kv_ref[lax.div(b, bpd), lax.rem(b, bpd)]


def lend(lists, recv, parts, cap, bpd):
    return pl.pallas_call(
        functools.partial(lend_kernel, parts, cap, bpd),
        out_shape=[jax.ShapeDtypeStruct((cap, BS, 2 * HD), bf16)] * (parts - 1),
        in_specs=[SMEM, VMEM],
        out_specs=[VMEM] * (parts - 1),
        compiler_params=params(),
        cost_estimate=cost(0, 2 * parts * cap * BS * 4 * HD),
        name="lend",
    )(lists, recv)


def attend_kernel(parts, cap, n, bpd, idx_ref, recv_ref, tau_ref, *refs):
    borrowed = refs[: parts - 1]
    dq_ref, own_ref = refs[parts - 1 : parts + 1]
    back = refs[parts + 1 : 2 * parts]
    tab, kt_tab, acc, s_buf, dp_buf, sem = refs[2 * parts :]
    nblk = n * bpd
    slots = (parts - 1) * cap
    copies = [
        pltpu.make_async_copy(recv_ref.at[j, pl.ds(0, bpd)], tab.at[pl.ds(j * bpd, bpd)], sem.at[j])
        for j in range(n)
    ]
    for k in range(1, parts):
        copies.append(
            pltpu.make_async_copy(borrowed[k - 1], tab.at[pl.ds(nblk + (k - 1) * cap, cap)], sem.at[n + k])
        )
    for c in copies:
        c.start()
    acc[...] = jnp.zeros_like(acc)
    for c in copies:
        c.wait()

    def flip(t, _):
        kt_tab[t] = tab[t].astype(f32).T[:HD].astype(bf16)
        return 0

    lax.fori_loop(0, nblk + slots, flip, 0)
    lane = lax.broadcasted_iota(jnp.int32, (BS, 2 * HD), 1)
    low = lane < HD
    zero = jnp.zeros((BS, 2 * HD), bf16)

    def one(r, g, rb):
        qg = recv_ref[g, bpd + rb]
        both = jnp.concatenate([jnp.where(low, qg, zero), jnp.where(low, zero, qg)], 0)
        top = None
        where = [idx_ref[r * NBR + i] for i in range(NBR)]
        for i in range(NBR):
            e = where[i]
            kv = tab[e]
            res = lax.dot_general(kv, both, (((1,), (1,)), ((), ())), preferred_element_type=f32)
            s = res[:, :BS]
            s_buf[rb, i] = s
            dp_buf[rb, i] = res[:, BS:]
            m8 = jnp.max(s.reshape(BS // 8, 8, BS), axis=0)
            top = m8 if top is None else jnp.maximum(top, m8)
        m = jnp.max(top, axis=0, keepdims=True)
        tau = tau_ref[pl.ds(r, 1), :]
        c = tau * LOG2E
        total = weighted = None
        for i in range(NBR):
            ex = jnp.exp2((s_buf[rb, i] - m) * c)
            s_buf[rb, i] = ex
            l8 = jnp.sum(ex.reshape(BS // 8, 8, BS), axis=0)
            d8 = jnp.sum((ex * dp_buf[rb, i]).reshape(BS // 8, 8, BS), axis=0)
            total = l8 if total is None else total + l8
            weighted = d8 if weighted is None else weighted + d8
        norm = jnp.sum(total, axis=0, keepdims=True)
        inv = 1.0 / norm
        delta = jnp.sum(weighted, axis=0, keepdims=True) * inv
        dq = None
        for i in range(0, NBR, 2):
            us = []
            for j in (i, i + 1):
                e = where[j]
                p = s_buf[rb, j] * inv
                u = (p * (dp_buf[rb, j] - delta) * tau).astype(bf16)
                us.append(u)
                part = jnp.dot(jnp.concatenate([u, p.astype(bf16)], 1), both, preferred_element_type=f32)
                acc[e] += part
            kt = jnp.concatenate([kt_tab[where[i]], kt_tab[where[i + 1]]], 1)
            d = jnp.dot(kt, jnp.concatenate(us, 0), preferred_element_type=f32)
            dq = d if dq is None else dq + d
        return dq

    def pair(g, _):
        dqs = [one(g * bpd + rb, g, rb) for rb in range(bpd)]
        dq_ref[g] = jnp.concatenate(dqs, 0).T.astype(bf16)
        return 0

    lax.fori_loop(0, n, pair, 0)
    own_ref[...] = acc[pl.ds(0, nblk)]
    for k in range(1, parts):
        back[k - 1][...] = acc[pl.ds(nblk + (k - 1) * cap, cap)].astype(bf16)


def attend(idx, recv, tau, borrowed, parts, cap, n, bpd):
    nblk = n * bpd
    slots = (parts - 1) * cap
    width = 2 * HD
    return pl.pallas_call(
        functools.partial(attend_kernel, parts, cap, n, bpd),
        out_shape=[
            jax.ShapeDtypeStruct((n, BS, width), bf16),
            jax.ShapeDtypeStruct((nblk, BS, width), f32),
        ]
        + [jax.ShapeDtypeStruct((cap, BS, width), bf16)] * (parts - 1),
        in_specs=[SMEM, VMEM, VMEM] + [VMEM] * (parts - 1),
        out_specs=[VMEM] * (parts + 1),
        scratch_shapes=[
            pltpu.VMEM((nblk + slots, BS, width), bf16),
            pltpu.VMEM((nblk + slots, HD, BS), bf16),
            pltpu.VMEM((nblk + slots, BS, width), f32),
            pltpu.VMEM((bpd, NBR, BS, BS), f32),
            pltpu.VMEM((bpd, NBR, BS, BS), f32),
            pltpu.SemaphoreType.DMA((n + parts,)),
        ],
        compiler_params=params(),
        cost_estimate=cost(nblk * NBR * BS * BS * HD * 2 * 5 * 2, 6 << 20),
        name="attend",
    )(idx, recv, tau, *borrowed)


def gather_kernel(parts, cap, bpd, lists_ref, dq_ref, own_ref, *refs):
    returned, out_ref, total = refs[: parts - 1], refs[parts - 1], refs[parts]
    n = dq_ref.shape[0]
    total[...] = own_ref[...]
    for k in range(1, parts):
        for s in range(cap):
            b = lists_ref[k * cap + s]
            total[b] += returned[k - 1][s].astype(f32)
    for j in range(n):
        out_ref[j, pl.ds(0, BS)] = dq_ref[j]
        for b in range(bpd):
            out_ref[j, pl.ds((1 + b) * BS, BS)] = total[j * bpd + b].astype(bf16)


def collect(lists, dq, own, returned, parts, cap, bpd):
    n = dq.shape[0]
    return pl.pallas_call(
        functools.partial(gather_kernel, parts, cap, bpd),
        out_shape=jax.ShapeDtypeStruct((n, (1 + bpd) * BS, 2 * HD), bf16),
        in_specs=[SMEM] + [VMEM] * (parts + 1),
        out_specs=VMEM,
        scratch_shapes=[pltpu.VMEM(own.shape, f32)],
        compiler_params=params(),
        cost_estimate=cost(0, 4 << 20),
        name="collect",
    )(lists, dq, own, *returned)


def unpack_kernel(n, phases, bpd, *refs):
    recv = refs[:phases]
    gq, gk, gv = refs[phases:]
    rows = bpd * BS
    for f in range(phases):
        for j in range(n):
            cols = pl.ds((f * n + j) * HD, HD)
            for b in range(bpd):
                gq[pl.ds(b * BS, BS), cols] = recv[f][j, pl.ds(0, BS), pl.ds(b * HD, HD)]
            gk[:, cols] = recv[f][j, pl.ds(BS, rows), pl.ds(0, HD)]
            gv[:, cols] = recv[f][j, pl.ds(BS, rows), pl.ds(HD, HD)]


def unpack(recv, n, bpd):
    rows = bpd * BS
    return pl.pallas_call(
        functools.partial(unpack_kernel, n, len(recv), bpd),
        out_shape=[jax.ShapeDtypeStruct((rows, D), bf16)] * 3,
        in_specs=[VMEM] * len(recv),
        out_specs=[VMEM] * 3,
        compiler_params=params(),
        cost_estimate=cost(0, 4 << 20),
        name="unpack",
    )(*recv)


def swap(x, k, parts):
    return lax.ppermute(x, "dom", [(i, i ^ k) for i in range(parts)])


def body(node_queries, node_keys, node_values, out_grad, degrees, neighbor_blocks, send_slots):
    n = lax.axis_size("head")
    parts = lax.axis_size("dom")
    cap = send_slots.shape[2]
    phases = H // n
    rows = node_queries.shape[0]
    bpd = rows // BS
    nblk = n * bpd
    me = lax.axis_index("dom")
    hop = jnp.arange(parts, dtype=jnp.int32)
    mine = jnp.maximum(lax.dynamic_index_in_dim(send_slots, me, 0, keepdims=False), 0)
    pick = (hop[:, None] == (hop[None, :] ^ me)).astype(jnp.int32)
    lists = jnp.sum(pick[:, :, None] * mine[None], axis=1).reshape(-1)
    away = neighbor_blocks - nblk
    moved = nblk + ((away // cap) ^ me) * cap + away % cap - cap
    idx = jnp.where(away < 0, neighbor_blocks, moved).reshape(-1)
    tau = (jnp.log(degrees.astype(f32)) / math.log(64.0) / math.sqrt(HD)).reshape(nblk, BS)

    sent = [pack(node_queries, node_keys, node_values, out_grad, f, n) for f in range(phases)]
    recv = []
    for f in range(phases):
        recv.append(
            lax.all_to_all(sent[f], "head", split_axis=0, concat_axis=0, tiled=True).reshape(
                n, 2 * bpd, BS, 2 * HD
            )
        )
    outs = []
    for f in range(phases):
        lent = lend(lists, recv[f], parts, cap, bpd)
        borrowed = [
            swap(lent[k - 1], k, parts) for k in range(1, parts)
        ]
        dq, own, *back = attend(idx, recv[f], tau, borrowed, parts, cap, n, bpd)
        returned = [swap(back[k - 1], k, parts) for k in range(1, parts)]
        total = collect(lists, dq, own, returned, parts, cap, bpd)
        outs.append(lax.all_to_all(total, "head", split_axis=0, concat_axis=0, tiled=True))
    return tuple(unpack(outs, n, bpd))


def solution(mesh):
    placed = (
        P(("dom", "head"), None),
        P(("dom", "head"), None),
        P(("dom", "head"), None),
        P(("dom", "head"), None),
        P("dom"),
        P("dom", None),
        P(),
    )
    return jax.shard_map(
        body,
        mesh=mesh,
        in_specs=placed,
        out_specs=(P(("dom", "head"), None), P(("dom", "head"), None), P(("dom", "head"), None)),
        check_vma=False,
    )
```

```python
import functools
import math

import jax
import jax.numpy as jnp
from jax import lax
from jax.experimental import pallas as pl
from jax.experimental.pallas import tpu as pltpu
from jax.sharding import PartitionSpec as P

D = 1024
H = 16
NBR = 12
BS = 128
HD = D // H
LOG2E = 1.4426950408889634
VMEM_LIMIT = 56 << 20

bf16 = jnp.bfloat16
f32 = jnp.float32


def params():
    return pltpu.CompilerParams(vmem_limit_bytes=VMEM_LIMIT)


def cost(flops, bytes_accessed):
    return pl.CostEstimate(flops=flops, bytes_accessed=bytes_accessed, transcendentals=0)


VMEM = pl.BlockSpec(memory_space=pltpu.VMEM)
SMEM = pl.BlockSpec(memory_space=pltpu.SMEM)
ANY = pl.BlockSpec(memory_space=pl.ANY)


def pack_kernel(first, count, n, x_ref, y_ref, out_ref):
    rows = x_ref.shape[0]
    for f in range(count):
        at = pl.ds(f * rows, rows)
        for j in range(n):
            cols = pl.ds(((first + f) * n + j) * HD, HD)
            out_ref[j, at, pl.ds(0, HD)] = x_ref[:, cols]
            out_ref[j, at, pl.ds(HD, HD)] = y_ref[:, cols]


def pack(x, y, first, count, n):
    rows = x.shape[0]
    return pl.pallas_call(
        functools.partial(pack_kernel, first, count, n),
        out_shape=jax.ShapeDtypeStruct((n, count * rows, 2 * HD), bf16),
        in_specs=[VMEM] * 2,
        out_specs=VMEM,
        compiler_params=params(),
        cost_estimate=cost(0, 8 * rows * D),
        name="pack",
    )(x, y)


def lend_kernel(phases, parts, cap, bpd, lists_ref, kv_ref, *outs):
    for k in range(1, parts):
        for s in range(cap):
            b = lists_ref[k * cap + s]
            j, o = lax.div(b, bpd), lax.rem(b, bpd)
            for f in range(phases):
                outs[k - 1][f * cap + s] = kv_ref[j, f * bpd + o]


def lend(lists, kv, phases, parts, cap, bpd):
    return pl.pallas_call(
        functools.partial(lend_kernel, phases, parts, cap, bpd),
        out_shape=[jax.ShapeDtypeStruct((phases * cap, BS, 2 * HD), bf16)] * (parts - 1),
        in_specs=[SMEM, VMEM],
        out_specs=[VMEM] * (parts - 1),
        compiler_params=params(),
        cost_estimate=cost(0, 4 * parts * cap * BS * 4 * HD),
        name="lend",
    )(lists, kv)


def attend_kernel(f, parts, cap, n, bpd, idx_ref, kv_ref, qg_ref, tau_ref, *refs):
    borrowed, refs = refs[: parts - 1], refs[parts - 1 :]
    earlier, refs = (refs[: parts - 1], refs[parts - 1 :]) if f else ((), refs)
    dq_ref, own_ref = refs[:2]
    back = refs[2 : parts + 1]
    tab, kt_tab, acc, s_buf, dp_buf, sem = refs[parts + 1 :]
    nblk = n * bpd
    slots = (parts - 1) * cap
    copies = [
        pltpu.make_async_copy(kv_ref.at[j, pl.ds(f * bpd, bpd)], tab.at[pl.ds(j * bpd, bpd)], sem.at[j])
        for j in range(n)
    ]
    for k in range(1, parts):
        copies.append(
            pltpu.make_async_copy(borrowed[k - 1].at[pl.ds(f * cap, cap)], tab.at[pl.ds(nblk + (k - 1) * cap, cap)], sem.at[n + k])
        )
    for c in copies:
        c.start()
    acc[...] = jnp.zeros_like(acc)
    for c in copies:
        c.wait()

    def flip(t, _):
        kt_tab[t] = tab[t].astype(f32).T[:HD].astype(bf16)
        return 0

    lax.fori_loop(0, nblk + slots, flip, 0, unroll=4)
    lane = lax.broadcasted_iota(jnp.int32, (BS, 2 * HD), 1)
    low = lane < HD
    zero = jnp.zeros((BS, 2 * HD), bf16)

    def fold8(x, op):
        return op(x.reshape(BS // 8, 8, BS), axis=0)

    def load(r):
        qg = qg_ref[lax.div(r, bpd), lax.rem(r, bpd)]
        both = jnp.concatenate([jnp.where(low, qg, zero), jnp.where(low, zero, qg)], 0)
        return both, [idx_ref[r * NBR + i] for i in range(NBR)]

    def step1(slot, both, where, i, top):
        rr = lax.dot_general(tab[where[i]], both, (((1,), (1,)), ((), ())), preferred_element_type=f32)
        s = rr[:, :BS]
        s_buf[slot, i] = s
        dp_buf[slot, i] = rr[:, BS:]
        m8 = fold8(s, jnp.max)
        return m8 if top is None else jnp.maximum(top, m8)

    def advance(r, slot, top, r2):
        both, where = load(r)
        both2, where2 = load(r2)
        m = jnp.max(top, axis=0, keepdims=True)
        tau = tau_ref[pl.ds(r, 1), :]
        c = tau * LOG2E
        top2 = None
        total = weighted = None
        nxt = 0
        for i in range(NBR):
            if i % 2 == 0:
                top2 = step1(1 - slot, both2, where2, nxt, top2); nxt += 1
            ex = jnp.exp2((s_buf[slot, i] - m) * c)
            s_buf[slot, i] = ex
            l8 = fold8(ex, jnp.sum)
            d8 = fold8(ex * dp_buf[slot, i], jnp.sum)
            total = l8 if total is None else total + l8
            weighted = d8 if weighted is None else weighted + d8
        norm = jnp.sum(total, axis=0, keepdims=True)
        inv = 1.0 / norm
        delta = jnp.sum(weighted, axis=0, keepdims=True) * inv
        dq = None
        for i in range(0, NBR, 2):
            us = []
            top2 = step1(1 - slot, both2, where2, nxt, top2); nxt += 1
            for j in (i, i + 1):
                p = s_buf[slot, j] * inv
                u = (p * (dp_buf[slot, j] - delta) * tau).astype(bf16)
                us.append(u)
                part = jnp.dot(jnp.concatenate([u, p.astype(bf16)], 1), both, preferred_element_type=f32)
                acc[where[j]] += part
            kt = jnp.concatenate([kt_tab[where[i]], kt_tab[where[i + 1]]], 1)
            d = jnp.dot(kt, jnp.concatenate(us, 0), preferred_element_type=f32)
            dq = d if dq is None else dq + d
        return dq, top2

    def pair(g, top):
        r = g * bpd
        dqs = []
        for rb in range(bpd):
            dq, top = advance(r + rb, rb % 2, top, jnp.minimum(r + rb + 1, nblk - 1))
            dqs.append(dq)
        dq_ref[g] = jnp.concatenate(dqs, 0).T.astype(bf16)
        return top
    both, where = load(0)
    top = None
    for i in range(NBR):
        top = step1(0, both, where, i, top)
    lax.fori_loop(0, n, pair, top)
    own_ref[...] = acc[pl.ds(0, nblk)]
    for k in range(1, parts):
        if f:
            back[k - 1][pl.ds(0, f * cap)] = earlier[k - 1][...]
        back[k - 1][pl.ds(f * cap, cap)] = acc[pl.ds(nblk + (k - 1) * cap, cap)].astype(bf16)


def attend(idx, kv, f, qg, tau, borrowed, earlier, parts, cap, n, bpd):
    nblk = n * bpd
    slots = (parts - 1) * cap
    width = 2 * HD
    return pl.pallas_call(
        functools.partial(attend_kernel, f, parts, cap, n, bpd),
        out_shape=[
            jax.ShapeDtypeStruct((n, BS, width), bf16),
            jax.ShapeDtypeStruct((nblk, BS, width), f32),
        ]
        + [jax.ShapeDtypeStruct(((f + 1) * cap, BS, width), bf16)] * (parts - 1),
        in_specs=[SMEM, VMEM, VMEM, VMEM] + [VMEM] * (len(borrowed) + len(earlier)),
        out_specs=[VMEM] * (parts + 1),
        scratch_shapes=[
            pltpu.VMEM((nblk + slots, BS, width), bf16),
            pltpu.VMEM((nblk + slots, HD, BS), bf16),
            pltpu.VMEM((nblk + slots, BS, width), f32),
            pltpu.VMEM((bpd, NBR, BS, BS), f32),
            pltpu.VMEM((bpd, NBR, BS, BS), f32),
            pltpu.SemaphoreType.DMA((n + parts,)),
        ],
        compiler_params=params(),
        cost_estimate=cost(nblk * NBR * BS * BS * HD * 100, 6 << 20),
        name="attend",
    )(idx, kv, qg, tau, *borrowed, *earlier)


def collect_kernel(phases, parts, cap, bpd, lists_ref, *refs):
    own, returned = refs[:phases], refs[phases : phases + parts - 1]
    out_ref, total = refs[phases + parts - 1 :]
    nblk = total.shape[0]
    for f in range(phases):
        total[...] = own[f][...]
        for k in range(1, parts):
            for s in range(cap):
                total[lists_ref[k * cap + s]] += returned[k - 1][f * cap + s].astype(f32)
        for b in range(nblk):
            out_ref[b // bpd, pl.ds((f * bpd + b % bpd) * BS, BS)] = total[b].astype(bf16)


def collect(lists, own, returned, phases, parts, cap, n, bpd):
    return pl.pallas_call(
        functools.partial(collect_kernel, phases, parts, cap, bpd),
        out_shape=jax.ShapeDtypeStruct((n, phases * bpd * BS, 2 * HD), bf16),
        in_specs=[SMEM] + [VMEM] * (phases + parts - 1),
        out_specs=VMEM,
        scratch_shapes=[pltpu.VMEM(own[0].shape, f32)],
        compiler_params=params(),
        cost_estimate=cost(0, 4 << 20),
        name="collect",
    )(lists, *own, *returned)


def unpack_kernel(n, phases, bpd, *refs):
    dqs, dkv = refs[:phases], refs[phases]
    gq, gk, gv = refs[phases + 1 :]
    rows = bpd * BS
    for f in range(phases):
        for j in range(n):
            cols = pl.ds((f * n + j) * HD, HD)
            for b in range(bpd):
                gq[pl.ds(b * BS, BS), cols] = dqs[f][j, :, pl.ds(b * HD, HD)]
            gk[:, cols] = dkv[j, pl.ds(f * rows, rows), pl.ds(0, HD)]
            gv[:, cols] = dkv[j, pl.ds(f * rows, rows), pl.ds(HD, HD)]


def unpack(dqs, dkv, n, bpd):
    rows = bpd * BS
    return pl.pallas_call(
        functools.partial(unpack_kernel, n, len(dqs), bpd),
        out_shape=[jax.ShapeDtypeStruct((rows, D), bf16)] * 3,
        in_specs=[VMEM] * (len(dqs) + 1),
        out_specs=[VMEM] * 3,
        compiler_params=params(),
        cost_estimate=cost(0, 4 << 20),
        name="unpack",
    )(*dqs, dkv)


def swap(x, k, parts):
    return lax.ppermute(x, "dom", [(i, i ^ k) for i in range(parts)])


def body(node_queries, node_keys, node_values, out_grad, degrees, neighbor_blocks, send_slots):
    n = lax.axis_size("head")
    parts = lax.axis_size("dom")
    cap = send_slots.shape[2]
    phases = H // n
    rows = node_queries.shape[0]
    bpd = rows // BS
    nblk = n * bpd
    me = lax.axis_index("dom")
    hop = jnp.arange(parts, dtype=jnp.int32)
    mine = jnp.maximum(lax.dynamic_index_in_dim(send_slots, me, 0, keepdims=False), 0)
    pick = (hop[:, None] == (hop[None, :] ^ me)).astype(jnp.int32)
    lists = jnp.sum(pick[:, :, None] * mine[None], axis=1).reshape(-1)
    away = neighbor_blocks - nblk
    moved = nblk + ((away // cap) ^ me) * cap + away % cap - cap
    idx = jnp.where(away < 0, neighbor_blocks, moved).reshape(-1)
    tau = (jnp.log(degrees.astype(f32)) / math.log(64.0) / math.sqrt(HD)).reshape(nblk, BS)

    def spread(x):
        return lax.all_to_all(x, "head", split_axis=0, concat_axis=0, tiled=True)

    kv = spread(pack(node_keys, node_values, 0, phases, n)).reshape(n, phases * bpd, BS, 2 * HD)
    sent = [pack(node_queries, out_grad, f, 1, n) for f in range(phases)]
    sent[0], kv = lax.optimization_barrier((sent[0], kv))
    qg = [spread(sent[0])]
    lent = lend(lists, kv, phases, parts, cap, bpd)
    borrowed = [swap(lent[k - 1], k, parts) for k in range(1, parts)]
    for f in range(1, phases):
        sent[f], qg[f - 1], borrowed = lax.optimization_barrier((sent[f], qg[f - 1], borrowed))
        qg.append(spread(sent[f]))
    dqs, owns, back = [], [], []
    for f in range(phases):
        block = qg[f].reshape(n, bpd, BS, 2 * HD)
        dq, own, *back = attend(idx, kv, f, block, tau, borrowed, back, parts, cap, n, bpd)
        if f + 1 < phases:
            dq, qg[f + 1] = lax.optimization_barrier((dq, qg[f + 1]))
        if f:
            dq, dqs[f - 1] = lax.optimization_barrier((dq, dqs[f - 1]))
        dqs.append(spread(dq))
        owns.append(own)
    returned = [swap(back[k - 1], k, parts) for k in range(1, parts)]
    total = collect(lists, owns, returned, phases, parts, cap, n, bpd)
    total, dqs = lax.optimization_barrier((total, dqs))
    return tuple(unpack(dqs, spread(total), n, bpd))


def solution(mesh):
    placed = (
        P(("dom", "head"), None),
        P(("dom", "head"), None),
        P(("dom", "head"), None),
        P(("dom", "head"), None),
        P("dom"),
        P("dom", None),
        P(),
    )
    return jax.shard_map(
        body,
        mesh=mesh,
        in_specs=placed,
        out_specs=(P(("dom", "head"), None), P(("dom", "head"), None), P(("dom", "head"), None)),
        check_vma=False,
    )
```

```python
import functools
import math

import jax
import jax.numpy as jnp
from jax import lax
from jax.experimental import pallas as pl
from jax.experimental.pallas import tpu as pltpu
from jax.sharding import PartitionSpec as P

D = 1024
H = 16
NBR = 12
BS = 128
HD = D // H
LOG2E = 1.4426950408889634
VMEM_LIMIT = 56 << 20

bf16 = jnp.bfloat16
f32 = jnp.float32


def params():
    return pltpu.CompilerParams(vmem_limit_bytes=VMEM_LIMIT)


def cost(flops, bytes_accessed):
    return pl.CostEstimate(flops=flops, bytes_accessed=bytes_accessed, transcendentals=0)


VMEM = pl.BlockSpec(memory_space=pltpu.VMEM)
SMEM = pl.BlockSpec(memory_space=pltpu.SMEM)
ANY = pl.BlockSpec(memory_space=pl.ANY)


def pack_kernel(first, n, x_ref, y_ref, out_ref):
    for j in range(n):
        cols = pl.ds((first * n + j) * HD, HD)
        out_ref[j, :, pl.ds(0, HD)] = x_ref[:, cols]
        out_ref[j, :, pl.ds(HD, HD)] = y_ref[:, cols]


def pack(x, y, first, n):
    rows = x.shape[0]
    return pl.pallas_call(
        functools.partial(pack_kernel, first, n),
        out_shape=jax.ShapeDtypeStruct((n, rows, 2 * HD), bf16),
        in_specs=[VMEM] * 2,
        out_specs=VMEM,
        compiler_params=params(),
        cost_estimate=cost(0, 8 * rows * D),
        name="pack",
    )(x, y)


def tile(at):
    return pl.ds(pl.multiple_of(at * 2 * HD, 2 * HD), 2 * HD)


def pieces_kernel(count, n, h_ref, x_ref, y_ref, *outs):
    rows = x_ref.shape[0]
    h = h_ref[0]
    odd = jnp.broadcast_to(h & 1, (rows, 2 * HD)) == 1
    for k in range(0, n, 2):
        for f in range(count):
            cols = tile(f * (n // 2) + ((h ^ k) >> 1))
            x, y = x_ref[:, cols], y_ref[:, cols]
            even_head = jnp.concatenate([x[:, :HD], y[:, :HD]], 1)
            odd_head = jnp.concatenate([x[:, HD:], y[:, HD:]], 1)
            at = pl.ds(f * rows, rows)
            outs[k][at] = jnp.where(odd, odd_head, even_head)
            outs[k + 1][at] = jnp.where(odd, even_head, odd_head)


def pieces(x, y, count, n, h):
    rows = x.shape[0]
    return pl.pallas_call(
        functools.partial(pieces_kernel, count, n),
        out_shape=[jax.ShapeDtypeStruct((count * rows, 2 * HD), bf16)] * n,
        in_specs=[SMEM] + [VMEM] * 2,
        out_specs=[VMEM] * n,
        compiler_params=params(),
        cost_estimate=cost(0, 8 * rows * D),
        name="pieces",
    )(h, x, y)


def lend_kernel(phases, parts, cap, bpd, lists_ref, *refs):
    outs = refs[-(parts - 1) :]
    kv_ref = refs[-parts]
    for k, piece in enumerate(refs[:-parts]):
        kv_ref[k] = piece[...]
    for k in range(1, parts):
        for s in range(cap):
            b = lists_ref[k * cap + s]
            j, o = lax.div(b, bpd), lax.rem(b, bpd)
            for f in range(phases):
                outs[k - 1][f * cap + s] = kv_ref[j, f * bpd + o]


def lend(lists, kv, phases, parts, cap, bpd):
    n = len(kv)
    return pl.pallas_call(
        functools.partial(lend_kernel, phases, parts, cap, bpd),
        out_shape=[jax.ShapeDtypeStruct((n, phases * bpd, BS, 2 * HD), bf16)]
        + [jax.ShapeDtypeStruct((phases * cap, BS, 2 * HD), bf16)] * (parts - 1),
        in_specs=[SMEM] + [VMEM] * n,
        out_specs=[VMEM] * parts,
        compiler_params=params(),
        cost_estimate=cost(0, 4 * parts * cap * BS * 4 * HD),
        name="lend",
    )(lists, *kv)


def attend_kernel(f, paired, parts, cap, n, bpd, idx_ref, h_ref, kv_ref, tau_ref, *refs):
    qg, refs = (refs[:n], refs[n:]) if paired else (refs[:1], refs[1:])
    h = h_ref[0]
    borrowed, refs = refs[: parts - 1], refs[parts - 1 :]
    dq_out, own_ref, refs = refs[0], refs[1], refs[2:]
    back = refs[: parts - 1]
    tab, qg_tab, kt_tab, acc, s_buf, dp_buf, sem = refs[parts - 1 :]
    nblk = n * bpd
    slots = (parts - 1) * cap
    copies = [
        pltpu.make_async_copy(kv_ref.at[j, pl.ds(f * bpd, bpd)], tab.at[pl.ds(j * bpd, bpd)], sem.at[j])
        for j in range(n)
    ]
    for k in range(1, parts):
        copies.append(
            pltpu.make_async_copy(borrowed[k - 1].at[pl.ds(f * cap, cap)], tab.at[pl.ds(nblk + (k - 1) * cap, cap)], sem.at[n + k])
        )
    for k in range(n):
        src = qg[k] if paired else qg[0].at[k ^ h]
        copies.append(pltpu.make_async_copy(src, qg_tab.at[pl.ds(k * bpd, bpd)], sem.at[n + parts + k]))
    for c in copies:
        c.start()
    acc[...] = jnp.zeros_like(acc)
    for c in copies:
        c.wait()

    def flip(t, _):
        kt_tab[t] = tab[t].astype(f32).T[:HD].astype(bf16)
        return 0

    lax.fori_loop(0, nblk + slots, flip, 0, unroll=4)
    lane = lax.broadcasted_iota(jnp.int32, (BS, 2 * HD), 1)
    low = lane < HD
    zero = jnp.zeros((BS, 2 * HD), bf16)

    def fold8(x, op):
        return op(x.reshape(BS // 8, 8, BS), axis=0)

    def load(r):
        qg = qg_tab[r]
        both = jnp.concatenate([jnp.where(low, qg, zero), jnp.where(low, zero, qg)], 0)
        return both, [idx_ref[r * NBR + i] for i in range(NBR)]

    def step1(slot, both, where, i, top):
        rr = lax.dot_general(tab[where[i]], both, (((1,), (1,)), ((), ())), preferred_element_type=f32)
        s = rr[:, :BS]
        s_buf[slot, i] = s
        dp_buf[slot, i] = rr[:, BS:]
        m8 = fold8(s, jnp.max)
        return m8 if top is None else jnp.maximum(top, m8)

    def advance(r, slot, top, r2):
        both, where = load(r)
        both2, where2 = load(r2)
        m = jnp.max(top, axis=0, keepdims=True)
        tau = tau_ref[pl.ds(r, 1), :]
        c = tau * LOG2E
        top2 = None
        total = weighted = None
        nxt = 0
        for i in range(NBR):
            if i % 2 == 0:
                top2 = step1(1 - slot, both2, where2, nxt, top2); nxt += 1
            ex = jnp.exp2((s_buf[slot, i] - m) * c)
            s_buf[slot, i] = ex
            l8 = fold8(ex, jnp.sum)
            d8 = fold8(ex * dp_buf[slot, i], jnp.sum)
            total = l8 if total is None else total + l8
            weighted = d8 if weighted is None else weighted + d8
        norm = jnp.sum(total, axis=0, keepdims=True)
        inv = 1.0 / norm
        delta = jnp.sum(weighted, axis=0, keepdims=True) * inv
        dq = None
        for i in range(0, NBR, 2):
            us = []
            top2 = step1(1 - slot, both2, where2, nxt, top2); nxt += 1
            for j in (i, i + 1):
                p = s_buf[slot, j] * inv
                u = (p * (dp_buf[slot, j] - delta) * tau).astype(bf16)
                us.append(u)
                part = jnp.dot(jnp.concatenate([u, p.astype(bf16)], 1), both, preferred_element_type=f32)
                acc[where[j]] += part
            kt = jnp.concatenate([kt_tab[where[i]], kt_tab[where[i + 1]]], 1)
            d = jnp.dot(kt, jnp.concatenate(us, 0), preferred_element_type=f32)
            dq = d if dq is None else dq + d
        return dq, top2

    def pair(g, top):
        r = g * bpd
        dqs = []
        for rb in range(bpd):
            dq, top = advance(r + rb, rb % 2, top, jnp.minimum(r + rb + 1, nblk - 1))
            dqs.append(dq)
        turned = jnp.concatenate(dqs, 0).T.astype(bf16)
        dq_out[g ^ h] = turned
        return top

    both, where = load(0)
    top = None
    for i in range(NBR):
        top = step1(0, both, where, i, top)
    lax.fori_loop(0, n, pair, top)
    own_ref[...] = acc[pl.ds(0, nblk)]
    for k in range(1, parts):
        back[k - 1][...] = acc[pl.ds(nblk + (k - 1) * cap, cap)].astype(bf16)


def attend(idx, h, kv, f, qg, tau, borrowed, parts, cap, n, bpd):
    nblk = n * bpd
    slots = (parts - 1) * cap
    width = 2 * HD
    paired = isinstance(qg, list)
    qg = qg if paired else [qg]
    out = pl.pallas_call(
        functools.partial(attend_kernel, f, paired, parts, cap, n, bpd),
        out_shape=[
            jax.ShapeDtypeStruct((n, BS, width), bf16),
            jax.ShapeDtypeStruct((nblk, BS, width), f32),
        ]
        + [jax.ShapeDtypeStruct((cap, BS, width), bf16)] * (parts - 1),
        in_specs=[SMEM, SMEM] + [VMEM] * (2 + len(qg) + len(borrowed)),
        out_specs=[VMEM] * (1 + parts),
        scratch_shapes=[
            pltpu.VMEM((nblk + slots, BS, width), bf16),
            pltpu.VMEM((nblk, BS, width), bf16),
            pltpu.VMEM((nblk + slots, HD, BS), bf16),
            pltpu.VMEM((nblk + slots, BS, width), f32),
            pltpu.VMEM((bpd, NBR, BS, BS), f32),
            pltpu.VMEM((bpd, NBR, BS, BS), f32),
            pltpu.SemaphoreType.DMA((2 * n + parts,)),
        ],
        compiler_params=params(),
        cost_estimate=cost(nblk * NBR * BS * BS * HD * 100, 6 << 20),
        name="attend",
    )(idx, h, kv, tau, *qg, *borrowed)
    return out[0], out[1], out[2:]


def collect_kernel(parts, cap, n, bpd, lists_ref, own, *refs):
    returned, outs, total = refs[: parts - 1], refs[parts - 1 : -1], refs[-1]
    total[...] = own[...]
    for k in range(1, parts):
        for s in range(cap):
            total[lists_ref[k * cap + s]] += returned[k - 1][s].astype(f32)
    for k in range(n):
        for b in range(bpd):
            outs[k][pl.ds(b * BS, BS)] = total[k * bpd + b].astype(bf16)


def collect(lists, own, returned, parts, cap, n, bpd):
    return pl.pallas_call(
        functools.partial(collect_kernel, parts, cap, n, bpd),
        out_shape=[jax.ShapeDtypeStruct((bpd * BS, 2 * HD), bf16)] * n,
        in_specs=[SMEM] + [VMEM] * parts,
        out_specs=[VMEM] * n,
        scratch_shapes=[pltpu.VMEM(own.shape, f32)],
        compiler_params=params(),
        cost_estimate=cost(0, 4 << 20),
        name="collect",
    )(lists, own, *returned)


def by_head(odd, one, two):
    low, high = jnp.where(odd, two, one), jnp.where(odd, one, two)
    return (
        jnp.concatenate([low[:, :HD], high[:, :HD]], 1),
        jnp.concatenate([low[:, HD:], high[:, HD:]], 1),
    )


def unpack_q_kernel(n, bpd, *refs):
    dqs, gq = refs[:-1], refs[-1]
    never = jnp.zeros((BS, 2 * HD), jnp.int32) == 1
    for f, dq in enumerate(dqs):
        for j in range(0, n, 2):
            for b, part in enumerate(by_head(never, dq[j], dq[j + 1])):
                gq[pl.ds(b * BS, BS), tile((f * n + j) // 2)] = part


def unpack_kv_kernel(n, phases, bpd, h_ref, *refs):
    dkv, gk, gv = refs[:-2], refs[-2], refs[-1]
    h = h_ref[0]
    rows = bpd * BS
    odd = jnp.broadcast_to(h & 1, (rows, 2 * HD)) == 1
    for f in range(phases):
        for k in range(0, n, 2):
            cols = tile(f * (n // 2) + ((h ^ k) >> 1))
            one, two = dkv[f * n + k], dkv[f * n + k + 1]
            gk[:, cols], gv[:, cols] = by_head(odd, one[...], two[...])


def unpack(kernel, count, name, rows, arrays):
    shape = jax.ShapeDtypeStruct((rows, D), bf16)
    return pl.pallas_call(
        kernel,
        out_shape=[shape] * count,
        in_specs=[VMEM if a.ndim > 1 else SMEM for a in arrays],
        out_specs=[VMEM] * count,
        compiler_params=params(),
        cost_estimate=cost(0, 4 << 20),
        name=name,
    )(*arrays)


def swap(x, k, axis, size):
    return lax.ppermute(x, axis, [(i, i ^ k) for i in range(size)])


def body(node_queries, node_keys, node_values, out_grad, degrees, neighbor_blocks, send_slots):
    n = lax.axis_size("head")
    parts = lax.axis_size("dom")
    cap = send_slots.shape[2]
    phases = H // n
    rows = node_queries.shape[0]
    bpd = rows // BS
    nblk = n * bpd
    me = lax.axis_index("dom")
    head = lax.axis_index("head")
    h = head.astype(jnp.int32).reshape(1)
    hop = jnp.arange(parts, dtype=jnp.int32)
    pick = (hop[:, None] == (hop[None, :] ^ me)).astype(jnp.int32)
    step = jnp.arange(n, dtype=jnp.int32)
    turn = (step[:, None] == (step[None, :] ^ head)).astype(jnp.int32)

    def local(b):
        return ((b // bpd) ^ head) * bpd + b % bpd

    def turned(x):
        y = x.reshape(n, -1)
        return jnp.sum(turn[:, :, None] * y[None], axis=1).reshape(x.shape)

    mine = jnp.maximum(lax.dynamic_index_in_dim(send_slots, me, 0, keepdims=False), 0)
    lists = local(jnp.sum(pick[:, :, None] * mine[None], axis=1).reshape(-1))
    away = neighbor_blocks - nblk
    moved = nblk + ((away // cap) ^ me) * cap + away % cap - cap
    idx = turned(jnp.where(away < 0, local(neighbor_blocks), moved)).reshape(-1)
    count = turned(degrees.reshape(nblk, BS))
    tau = jnp.log(count.astype(f32)) / math.log(64.0) / math.sqrt(HD)

    def spread(x):
        return lax.all_to_all(x, "head", split_axis=0, concat_axis=0, tiled=True)

    def trade(x):
        return [x[0]] + [swap(x[k], k, "head", n) for k in range(1, n)]

    kv = [x.reshape(phases * bpd, BS, 2 * HD) for x in trade(pieces(node_keys, node_values, phases, n, h))]
    sent = pieces(node_queries, out_grad, 1, n, h)
    qg = [[x.reshape(bpd, BS, 2 * HD) for x in trade(sent)]]
    kv_all, *lent = lend(lists, kv, phases, parts, cap, bpd)
    borrowed = [swap(lent[k - 1], k, "dom", parts) for k in range(1, parts)]
    for f in range(1, phases):
        sent, qg[f - 1], borrowed = lax.optimization_barrier(
            (pack(node_queries, out_grad, f, n), qg[f - 1], borrowed)
        )
        qg.append(spread(sent).reshape(n, bpd, BS, 2 * HD))
    dqs, total, owns, returns = [], [], [], []
    for f in range(phases):
        dq, own, back = attend(idx, h, kv_all, f, qg[f], tau, borrowed, parts, cap, n, bpd)
        if f + 1 < phases:
            dq, qg[f + 1] = lax.optimization_barrier((dq, qg[f + 1]))
        if f:
            dq, own, back, dqs[f - 1], returns[f - 1], owns[f - 1] = lax.optimization_barrier(
                (dq, own, back, dqs[f - 1], returns[f - 1], owns[f - 1])
            )
        dqs.append(spread(dq))
        owns.append(own)
        returns.append([swap(back[k - 1], k, "dom", parts) for k in range(1, parts)])
    for f in range(phases):
        total += trade(collect(lists, owns[f], returns[f], parts, cap, n, bpd))
    (grad_q,) = unpack(functools.partial(unpack_q_kernel, n, bpd), 1, "unpack_q", rows, dqs)
    grad_k, grad_v = unpack(
        functools.partial(unpack_kv_kernel, n, phases, bpd), 2, "unpack_kv", rows, [h, *total]
    )
    return grad_q, grad_k, grad_v


def solution(mesh):
    placed = (
        P(("dom", "head"), None),
        P(("dom", "head"), None),
        P(("dom", "head"), None),
        P(("dom", "head"), None),
        P("dom"),
        P("dom", None),
        P(),
    )
    return jax.shard_map(
        body,
        mesh=mesh,
        in_specs=placed,
        out_specs=(P(("dom", "head"), None), P(("dom", "head"), None), P(("dom", "head"), None)),
        check_vma=False,
    )
```

```python
import functools
import math

import jax
import jax.numpy as jnp
from jax import lax
from jax.experimental import pallas as pl
from jax.experimental.pallas import tpu as pltpu
from jax.sharding import PartitionSpec as P

D = 1024
H = 16
NBR = 12
BS = 128
HD = D // H
LOG2E = 1.4426950408889634
VMEM_LIMIT = 56 << 20

bf16 = jnp.bfloat16
f32 = jnp.float32


def params():
    return pltpu.CompilerParams(vmem_limit_bytes=VMEM_LIMIT)


def cost(flops, bytes_accessed):
    return pl.CostEstimate(flops=flops, bytes_accessed=bytes_accessed, transcendentals=0)


VMEM = pl.BlockSpec(memory_space=pltpu.VMEM)
SMEM = pl.BlockSpec(memory_space=pltpu.SMEM)
ANY = pl.BlockSpec(memory_space=pl.ANY)


def pack_kernel(first, n, q_ref, k_ref, v_ref, g_ref, out_ref):
    rows = q_ref.shape[0]
    for i in range(0, n, 2):
        cols = tile((first * n + i) // 2)
        for at, (x, y) in ((0, (k_ref[:, cols], v_ref[:, cols])), (rows, (q_ref[:, cols], g_ref[:, cols]))):
            out_ref[i, pl.ds(at, rows)] = jnp.concatenate([x[:, :HD], y[:, :HD]], 1)
            out_ref[i + 1, pl.ds(at, rows)] = jnp.concatenate([x[:, HD:], y[:, HD:]], 1)


def pack(queries, keys, values, grads, first, n):
    rows = queries.shape[0]
    return pl.pallas_call(
        functools.partial(pack_kernel, first, n),
        out_shape=jax.ShapeDtypeStruct((n, 2 * rows, 2 * HD), bf16),
        in_specs=[VMEM] * 4,
        out_specs=VMEM,
        compiler_params=params(),
        cost_estimate=cost(0, 8 * rows * D),
        name="pack",
    )(queries, keys, values, grads)


def tile(at):
    return pl.ds(pl.multiple_of(at * 2 * HD, 2 * HD), 2 * HD)


def pack_one_kernel(n, x_ref, y_ref, out_ref):
    for i in range(0, n, 2):
        cols = tile(i // 2)
        x, y = x_ref[:, cols], y_ref[:, cols]
        out_ref[i] = jnp.concatenate([x[:, :HD], y[:, :HD]], 1)
        out_ref[i + 1] = jnp.concatenate([x[:, HD:], y[:, HD:]], 1)


def pack_one(x, y, n):
    rows = x.shape[0]
    return pl.pallas_call(
        functools.partial(pack_one_kernel, n),
        out_shape=jax.ShapeDtypeStruct((n, rows, 2 * HD), bf16),
        in_specs=[VMEM] * 2,
        out_specs=VMEM,
        compiler_params=params(),
        cost_estimate=cost(0, 8 * rows * D),
        name="pack_one",
    )(x, y)


def pieces_kernel(n, h_ref, x_ref, y_ref, *outs):
    rows = x_ref.shape[0]
    h = h_ref[0]
    odd = jnp.broadcast_to(h & 1, (rows, 2 * HD)) == 1
    for k in range(0, n, 2):
        cols = tile((h ^ k) >> 1)
        x, y = x_ref[:, cols], y_ref[:, cols]
        even_head = jnp.concatenate([x[:, :HD], y[:, :HD]], 1)
        odd_head = jnp.concatenate([x[:, HD:], y[:, HD:]], 1)
        outs[k][...] = jnp.where(odd, odd_head, even_head)
        outs[k + 1][...] = jnp.where(odd, even_head, odd_head)


def pieces(x, y, n, h):
    rows = x.shape[0]
    return pl.pallas_call(
        functools.partial(pieces_kernel, n),
        out_shape=[jax.ShapeDtypeStruct((rows, 2 * HD), bf16)] * n,
        in_specs=[SMEM] + [VMEM] * 2,
        out_specs=[VMEM] * n,
        compiler_params=params(),
        cost_estimate=cost(0, 8 * rows * D),
        name="pieces",
    )(h, x, y)


def lend_kernel(parts, cap, bpd, lists_ref, h_ref, *refs):
    outs = refs[-(parts - 1) :]
    kvs = refs[: -(parts - 1)]
    h = h_ref[0]
    if len(kvs) > 1:
        source, h = kvs[-1], 0
        for k, piece in enumerate(kvs[:-1]):
            source[k] = piece[...]
    else:
        source = kvs[0]
    for k in range(1, parts):
        for s in range(cap):
            b = lists_ref[k * cap + s]
            outs[k - 1][s] = source[lax.div(b, bpd) ^ h, lax.rem(b, bpd)]


def lend(lists, h, kv, parts, cap, bpd):
    whole = [] if len(kv) == 1 else [jax.ShapeDtypeStruct((len(kv), bpd, BS, 2 * HD), bf16)]
    return pl.pallas_call(
        functools.partial(lend_kernel, parts, cap, bpd),
        out_shape=whole + [jax.ShapeDtypeStruct((cap, BS, 2 * HD), bf16)] * (parts - 1),
        in_specs=[SMEM, SMEM] + [VMEM] * len(kv),
        out_specs=[VMEM] * (len(whole) + parts - 1),
        compiler_params=params(),
        cost_estimate=cost(0, 4 * parts * cap * BS * 4 * HD),
        name="lend",
    )(lists, h, *kv)


def attend_kernel(paired, parts, cap, n, bpd, idx_ref, h_ref, kv_ref, tau_ref, *refs):
    qg, refs = (refs[0], refs[1:]) if paired else (None, refs)
    h = h_ref[0]
    borrowed, refs = refs[: parts - 1], refs[parts - 1 :]
    dq_out, own_ref, refs = refs[0], refs[1], refs[2:]
    back = refs[: parts - 1]
    tab, qg_tab, kt_tab, acc, s_buf, dp_buf, sem = refs[parts - 1 :]
    nblk = n * bpd
    slots = (parts - 1) * cap
    copies = []
    for k in range(n):
        j = k if paired else k ^ h
        src = qg.at[k ^ h] if paired else kv_ref.at[j, pl.ds(bpd, bpd)]
        copies.append(pltpu.make_async_copy(kv_ref.at[j, pl.ds(0, bpd)], tab.at[pl.ds(k * bpd, bpd)], sem.at[k]))
        copies.append(pltpu.make_async_copy(src, qg_tab.at[pl.ds(k * bpd, bpd)], sem.at[n + parts + k]))
    for k in range(1, parts):
        copies.append(
            pltpu.make_async_copy(borrowed[k - 1], tab.at[pl.ds(nblk + (k - 1) * cap, cap)], sem.at[n + k])
        )
    for c in copies:
        c.start()
    acc[...] = jnp.zeros_like(acc)
    for c in copies:
        c.wait()

    def flip(t, _):
        kt_tab[t] = tab[t].astype(f32).T[:HD].astype(bf16)
        return 0

    lax.fori_loop(0, nblk + slots, flip, 0, unroll=4)
    lane = lax.broadcasted_iota(jnp.int32, (BS, 2 * HD), 1)
    low = lane < HD
    zero = jnp.zeros((BS, 2 * HD), bf16)

    def fold8(x, op):
        return op(x.reshape(BS // 8, 8, BS), axis=0)

    def load(r):
        qg = qg_tab[r]
        both = jnp.concatenate([jnp.where(low, qg, zero), jnp.where(low, zero, qg)], 0)
        return both, [idx_ref[r * NBR + i] for i in range(NBR)]

    def step1(slot, both, where, i, top):
        rr = lax.dot_general(tab[where[i]], both, (((1,), (1,)), ((), ())), preferred_element_type=f32)
        s = rr[:, :BS]
        s_buf[slot, i] = s
        dp_buf[slot, i] = rr[:, BS:]
        m8 = fold8(s, jnp.max)
        return m8 if top is None else jnp.maximum(top, m8)

    def advance(r, slot, top, r2):
        both, where = load(r)
        both2, where2 = load(r2)
        m = jnp.max(top, axis=0, keepdims=True)
        tau = tau_ref[pl.ds(r, 1), :]
        c = tau * LOG2E
        top2 = None
        total = weighted = None
        nxt = 0
        for i in range(NBR):
            if i % 2 == 0:
                top2 = step1(1 - slot, both2, where2, nxt, top2); nxt += 1
            ex = jnp.exp2((s_buf[slot, i] - m) * c)
            s_buf[slot, i] = ex
            l8 = fold8(ex, jnp.sum)
            d8 = fold8(ex * dp_buf[slot, i], jnp.sum)
            total = l8 if total is None else total + l8
            weighted = d8 if weighted is None else weighted + d8
        norm = jnp.sum(total, axis=0, keepdims=True)
        inv = 1.0 / norm
        delta = jnp.sum(weighted, axis=0, keepdims=True) * inv
        dq = None
        for i in range(0, NBR, 2):
            us = []
            top2 = step1(1 - slot, both2, where2, nxt, top2); nxt += 1
            for j in (i, i + 1):
                p = s_buf[slot, j] * inv
                u = (p * (dp_buf[slot, j] - delta) * tau).astype(bf16)
                us.append(u)
                part = jnp.dot(jnp.concatenate([u, p.astype(bf16)], 1), both, preferred_element_type=f32)
                acc[where[j]] += part
            kt = jnp.concatenate([kt_tab[where[i]], kt_tab[where[i + 1]]], 1)
            d = jnp.dot(kt, jnp.concatenate(us, 0), preferred_element_type=f32)
            dq = d if dq is None else dq + d
        return dq, top2

    def pair(g, top):
        r = g * bpd
        dqs = []
        for rb in range(bpd):
            dq, top = advance(r + rb, rb % 2, top, jnp.minimum(r + rb + 1, nblk - 1))
            dqs.append(dq)
        turned = jnp.concatenate(dqs, 0).T.astype(bf16)
        dq_out[g ^ h] = turned
        return top

    both, where = load(0)
    top = None
    for i in range(NBR):
        top = step1(0, both, where, i, top)
    lax.fori_loop(0, n, pair, top)
    own_ref[...] = acc[pl.ds(0, nblk)]
    for k in range(1, parts):
        back[k - 1][...] = acc[pl.ds(nblk + (k - 1) * cap, cap)].astype(bf16)


def attend(idx, h, kv, qg, tau, borrowed, parts, cap, n, bpd):
    nblk = n * bpd
    slots = (parts - 1) * cap
    width = 2 * HD
    out = pl.pallas_call(
        functools.partial(attend_kernel, bool(qg), parts, cap, n, bpd),
        out_shape=[
            jax.ShapeDtypeStruct((n, BS, width), bf16),
            jax.ShapeDtypeStruct((nblk, BS, width), f32),
        ]
        + [jax.ShapeDtypeStruct((cap, BS, width), bf16)] * (parts - 1),
        in_specs=[SMEM, SMEM] + [VMEM] * (2 + len(qg) + len(borrowed)),
        out_specs=[VMEM] * (1 + parts),
        scratch_shapes=[
            pltpu.VMEM((nblk + slots, BS, width), bf16),
            pltpu.VMEM((nblk, BS, width), bf16),
            pltpu.VMEM((nblk + slots, HD, BS), bf16),
            pltpu.VMEM((nblk + slots, BS, width), f32),
            pltpu.VMEM((bpd, NBR, BS, BS), f32),
            pltpu.VMEM((bpd, NBR, BS, BS), f32),
            pltpu.SemaphoreType.DMA((2 * n + parts,)),
        ],
        compiler_params=params(),
        cost_estimate=cost(nblk * NBR * BS * BS * HD * 100, 6 << 20),
        name="attend",
    )(idx, h, kv, tau, *qg, *borrowed)
    return out[0], out[1], out[2:]


def collect_kernel(last, parts, cap, n, bpd, lists_ref, h_ref, own, *refs):
    returned, refs = refs[: parts - 1], refs[parts - 1 :]
    total = refs[-1]
    total[...] = own[...]
    for k in range(1, parts):
        for s in range(cap):
            total[lists_ref[k * cap + s]] += returned[k - 1][s].astype(f32)
    if not last:
        dq, out = refs[0], refs[1]
        out[:, pl.ds(0, BS)] = dq[...]
    for k in range(n):
        for b in range(bpd):
            block = total[k * bpd + b].astype(bf16)
            if last:
                refs[k][pl.ds(b * BS, BS)] = block
            else:
                out[k ^ h_ref[0], pl.ds((1 + b) * BS, BS)] = block


def collect(lists, h, own, returned, dq, parts, cap, n, bpd):
    last = dq is None
    if last:
        out = [jax.ShapeDtypeStruct((bpd * BS, 2 * HD), bf16)] * n
    else:
        out = [jax.ShapeDtypeStruct((n, (1 + bpd) * BS, 2 * HD), bf16)]
    more = [] if last else [dq]
    return pl.pallas_call(
        functools.partial(collect_kernel, last, parts, cap, n, bpd),
        out_shape=out,
        in_specs=[SMEM, SMEM] + [VMEM] * (parts + len(more)),
        out_specs=[VMEM] * len(out),
        scratch_shapes=[pltpu.VMEM(own.shape, f32)],
        compiler_params=params(),
        cost_estimate=cost(0, 4 << 20),
        name="collect",
    )(lists, h, own, *returned, *more)


def by_head(odd, one, two):
    low, high = jnp.where(odd, two, one), jnp.where(odd, one, two)
    return (
        jnp.concatenate([low[:, :HD], high[:, :HD]], 1),
        jnp.concatenate([low[:, HD:], high[:, HD:]], 1),
    )


def unpack_early_kernel(n, bpd, *refs):
    *arrived, last_q, gq, gk, gv = refs
    rows = bpd * BS
    never = jnp.zeros((rows, 2 * HD), jnp.int32) == 1
    never_q = jnp.zeros((BS, 2 * HD), jnp.int32) == 1
    top, tail = pl.ds(0, BS), pl.ds(BS, rows)
    for f, got in enumerate([*arrived, last_q]):
        for j in range(0, n, 2):
            cols = tile((f * n + j) // 2)
            for b, part in enumerate(by_head(never_q, got[j, top], got[j + 1, top])):
                gq[pl.ds(b * BS, BS), cols] = part
            if f < len(arrived):
                gk[:, cols], gv[:, cols] = by_head(never, got[j, tail], got[j + 1, tail])


def unpack_last_kernel(n, h_ref, *refs):
    last, gk, gv = refs[:n], refs[-2], refs[-1]
    h = h_ref[0]
    odd = jnp.broadcast_to(h & 1, last[0].shape) == 1
    for k in range(0, n, 2):
        cols = tile((h ^ k) >> 1)
        gk[:, cols], gv[:, cols] = by_head(odd, last[k][...], last[k + 1][...])


def unpack(arrived, last_q, total, h, phases, n, bpd):
    rows = bpd * BS
    shape = jax.ShapeDtypeStruct((rows, D), bf16)
    gq, gk, gv = pl.pallas_call(
        functools.partial(unpack_early_kernel, n, bpd),
        out_shape=[shape] * 3,
        in_specs=[VMEM] * (len(arrived) + 1),
        out_specs=[VMEM] * 3,
        compiler_params=params(),
        cost_estimate=cost(0, 8 << 20),
        name="unpack_early",
    )(*arrived, last_q)
    part = pl.BlockSpec((rows, n * HD), lambda i: (0, phases - 1))
    gk, gv = pl.pallas_call(
        functools.partial(unpack_last_kernel, n),
        grid=(1,),
        out_shape=[shape] * 2,
        in_specs=[SMEM] + [VMEM] * n + [ANY] * 2,
        out_specs=[part] * 2,
        input_output_aliases={n + 1: 0, n + 2: 1},
        compiler_params=params(),
        cost_estimate=cost(0, 2 << 20),
        name="unpack_last",
    )(h, *total, gk, gv)
    return gq, gk, gv


def swap(x, k, axis, size):
    return lax.ppermute(x, axis, [(i, i ^ k) for i in range(size)])


def body(node_queries, node_keys, node_values, out_grad, degrees, neighbor_blocks, send_slots):
    n = lax.axis_size("head")
    parts = lax.axis_size("dom")
    cap = send_slots.shape[2]
    phases = H // n
    rows = node_queries.shape[0]
    bpd = rows // BS
    nblk = n * bpd
    me = lax.axis_index("dom")
    head = lax.axis_index("head")
    h = head.astype(jnp.int32).reshape(1)
    hop = jnp.arange(parts, dtype=jnp.int32)
    pick = (hop[:, None] == (hop[None, :] ^ me)).astype(jnp.int32)
    step = jnp.arange(n, dtype=jnp.int32)
    turn = (step[:, None] == (step[None, :] ^ head)).astype(jnp.int32)

    def local(b):
        return ((b // bpd) ^ head) * bpd + b % bpd

    def turned(x):
        y = x.reshape(n, -1)
        return jnp.sum(turn[:, :, None] * y[None], axis=1).reshape(x.shape)

    mine = jnp.maximum(lax.dynamic_index_in_dim(send_slots, me, 0, keepdims=False), 0)
    lists = local(jnp.sum(pick[:, :, None] * mine[None], axis=1).reshape(-1))
    away = neighbor_blocks - nblk
    moved = nblk + ((away // cap) ^ me) * cap + away % cap - cap
    idx = turned(jnp.where(away < 0, local(neighbor_blocks), moved)).reshape(-1)
    count = turned(degrees.reshape(nblk, BS))
    tau = jnp.log(count.astype(f32)) / math.log(64.0) / math.sqrt(HD)

    def spread(x):
        return lax.all_to_all(x, "head", split_axis=0, concat_axis=0, tiled=True)

    def trade(x):
        return [x[0]] + [swap(x[k], k, "head", n) for k in range(1, n)]

    kv = [x.reshape(bpd, BS, 2 * HD) for x in trade(pieces(node_keys, node_values, n, h))]
    early = 1 + n // 4
    first, kv[1:early] = lax.optimization_barrier((pack_one(node_queries, out_grad, n), kv[1:early]))
    qg = [spread(first).reshape(n, bpd, BS, 2 * HD)]
    later = []
    for f in range(1, phases):
        sent, qg = lax.optimization_barrier((pack(node_queries, node_keys, node_values, out_grad, f, n), qg))
        later.append(spread(sent).reshape(n, 2 * bpd, BS, 2 * HD))
    arrived, total, sent = [], [], None
    for f in range(phases):
        last = f + 1 == phases
        if f:
            kv, qg = [later[f - 1]], []
        lent = lend(lists, h, kv, parts, cap, bpd)
        borrowed = [swap(x, k + 1, "dom", parts) for k, x in enumerate(lent[-(parts - 1) :])]
        if f:
            borrowed, _ = lax.optimization_barrier((borrowed, sent))
            arrived.append(spread(sent))
        dq, own, back = attend(idx, h, lent[0] if f == 0 else kv[0], qg, tau, borrowed, parts, cap, n, bpd)
        returned = [swap(back[k - 1], k, "dom", parts) for k in range(1, parts)]
        if f:
            dq, arrived[-1], returned = lax.optimization_barrier((dq, arrived[-1], returned))
        if last:
            dq_all = spread(dq)
        out = collect(lists, h, own, returned, None if last else dq, parts, cap, n, bpd)
        if last:
            total = trade(out)
        else:
            sent = out[0]
    return tuple(unpack(arrived, dq_all, total, h, phases, n, bpd))


def solution(mesh):
    placed = (
        P(("dom", "head"), None),
        P(("dom", "head"), None),
        P(("dom", "head"), None),
        P(("dom", "head"), None),
        P("dom"),
        P("dom", None),
        P(),
    )
    return jax.shard_map(
        body,
        mesh=mesh,
        in_specs=placed,
        out_specs=(P(("dom", "head"), None), P(("dom", "head"), None), P(("dom", "head"), None)),
        check_vma=False,
    )
```

```python
import functools
import math

import jax
import jax.numpy as jnp
from jax import lax
from jax.experimental import pallas as pl
from jax.experimental.pallas import tpu as pltpu
from jax.sharding import PartitionSpec as P

D = 1024
H = 16
NBR = 12
BS = 128
HD = D // H
LOG2E = 1.4426950408889634
VMEM_LIMIT = 56 << 20

bf16 = jnp.bfloat16
f32 = jnp.float32


def params():
    return pltpu.CompilerParams(vmem_limit_bytes=VMEM_LIMIT)


def cost(flops, bytes_accessed):
    return pl.CostEstimate(flops=flops, bytes_accessed=bytes_accessed, transcendentals=0)


VMEM = pl.BlockSpec(memory_space=pltpu.VMEM)
SMEM = pl.BlockSpec(memory_space=pltpu.SMEM)
ANY = pl.BlockSpec(memory_space=pl.ANY)


def pack_kernel(first, n, q_ref, k_ref, v_ref, g_ref, out_ref):
    rows = q_ref.shape[0]
    for i in range(0, n, 2):
        cols = tile((first * n + i) // 2)
        for at, (x, y) in ((0, (k_ref[:, cols], v_ref[:, cols])), (rows, (q_ref[:, cols], g_ref[:, cols]))):
            out_ref[i, pl.ds(at, rows)] = jnp.concatenate([x[:, :HD], y[:, :HD]], 1)
            out_ref[i + 1, pl.ds(at, rows)] = jnp.concatenate([x[:, HD:], y[:, HD:]], 1)


def pack(queries, keys, values, grads, first, n):
    rows = queries.shape[0]
    return pl.pallas_call(
        functools.partial(pack_kernel, first, n),
        out_shape=jax.ShapeDtypeStruct((n, 2 * rows, 2 * HD), bf16),
        in_specs=[VMEM] * 4,
        out_specs=VMEM,
        compiler_params=params(),
        cost_estimate=cost(0, 8 * rows * D),
        name="pack",
    )(queries, keys, values, grads)


def tile(at):
    return pl.ds(pl.multiple_of(at * 2 * HD, 2 * HD), 2 * HD)


def pack_one_kernel(n, x_ref, y_ref, out_ref):
    for i in range(0, n, 2):
        cols = tile(i // 2)
        x, y = x_ref[:, cols], y_ref[:, cols]
        out_ref[i] = jnp.concatenate([x[:, :HD], y[:, :HD]], 1)
        out_ref[i + 1] = jnp.concatenate([x[:, HD:], y[:, HD:]], 1)


def pack_one(x, y, n):
    rows = x.shape[0]
    return pl.pallas_call(
        functools.partial(pack_one_kernel, n),
        out_shape=jax.ShapeDtypeStruct((n, rows, 2 * HD), bf16),
        in_specs=[VMEM] * 2,
        out_specs=VMEM,
        compiler_params=params(),
        cost_estimate=cost(0, 8 * rows * D),
        name="pack_one",
    )(x, y)


def pieces_kernel(n, h_ref, x_ref, y_ref, *outs):
    rows = x_ref.shape[0]
    h = h_ref[0]
    odd = jnp.broadcast_to(h & 1, (rows, 2 * HD)) == 1
    for k in range(0, n, 2):
        cols = tile((h ^ k) >> 1)
        x, y = x_ref[:, cols], y_ref[:, cols]
        even_head = jnp.concatenate([x[:, :HD], y[:, :HD]], 1)
        odd_head = jnp.concatenate([x[:, HD:], y[:, HD:]], 1)
        outs[k][...] = jnp.where(odd, odd_head, even_head)
        outs[k + 1][...] = jnp.where(odd, even_head, odd_head)


def pieces(x, y, n, h):
    rows = x.shape[0]
    return pl.pallas_call(
        functools.partial(pieces_kernel, n),
        out_shape=[jax.ShapeDtypeStruct((rows, 2 * HD), bf16)] * n,
        in_specs=[SMEM] + [VMEM] * 2,
        out_specs=[VMEM] * n,
        compiler_params=params(),
        cost_estimate=cost(0, 8 * rows * D),
        name="pieces",
    )(h, x, y)


def lend_kernel(parts, cap, bpd, lists_ref, h_ref, *refs):
    outs = refs[-(parts - 1) :]
    kvs = refs[: -(parts - 1)]
    h = h_ref[0]
    if len(kvs) > 1:
        source, h = kvs[-1], 0
        for k, piece in enumerate(kvs[:-1]):
            source[k] = piece[...]
    else:
        source = kvs[0]
    for k in range(1, parts):
        for s in range(cap):
            b = lists_ref[k * cap + s]
            outs[k - 1][s] = source[lax.div(b, bpd) ^ h, lax.rem(b, bpd)]


def lend(lists, h, kv, parts, cap, bpd):
    whole = [] if len(kv) == 1 else [jax.ShapeDtypeStruct((len(kv), bpd, BS, 2 * HD), bf16)]
    return pl.pallas_call(
        functools.partial(lend_kernel, parts, cap, bpd),
        out_shape=whole + [jax.ShapeDtypeStruct((cap, BS, 2 * HD), bf16)] * (parts - 1),
        in_specs=[SMEM, SMEM] + [VMEM] * len(kv),
        out_specs=[VMEM] * (len(whole) + parts - 1),
        compiler_params=params(),
        cost_estimate=cost(0, 4 * parts * cap * BS * 4 * HD),
        name="lend",
    )(lists, h, *kv)


def attend_kernel(paired, parts, cap, n, bpd, idx_ref, h_ref, kv_ref, tau_ref, *refs):
    qg, refs = (refs[0], refs[1:]) if paired else (None, refs)
    h = h_ref[0]
    borrowed, refs = refs[: parts - 1], refs[parts - 1 :]
    dq_out, own_ref, refs = refs[0], refs[1], refs[2:]
    back = refs[: parts - 1]
    tab, kt_tab, acc, s_buf, dp_buf = refs[parts - 1 :]
    nblk = n * bpd
    slots = (parts - 1) * cap

    def enter(t, block):
        tab[t] = block
        kt_tab[t] = block.astype(f32).T[:HD].astype(bf16)

    acc[...] = jnp.zeros_like(acc)
    for k in range(n):
        for b in range(bpd):
            enter(k * bpd + b, kv_ref[k if paired else k ^ h, b])
    for k in range(1, parts):
        for b in range(cap):
            enter(nblk + (k - 1) * cap + b, borrowed[k - 1][b])
    lane = lax.broadcasted_iota(jnp.int32, (BS, 2 * HD), 1)
    low = lane < HD
    zero = jnp.zeros((BS, 2 * HD), bf16)

    def fold8(x, op):
        return op(x.reshape(BS // 8, 8, BS), axis=0)

    def load(r):
        at, row = lax.div(r, bpd) ^ h, lax.rem(r, bpd)
        block = qg[at, row] if paired else kv_ref[at, bpd + row]
        both = jnp.concatenate([jnp.where(low, block, zero), jnp.where(low, zero, block)], 0)
        return both, [idx_ref[r * NBR + i] for i in range(NBR)]

    def step1(slot, both, where, i, top):
        rr = lax.dot_general(tab[where[i]], both, (((1,), (1,)), ((), ())), preferred_element_type=f32)
        s = rr[:, :BS]
        s_buf[slot, i] = s
        dp_buf[slot, i] = rr[:, BS:]
        m8 = fold8(s, jnp.max)
        return m8 if top is None else jnp.maximum(top, m8)

    def advance(r, slot, top, r2):
        both, where = load(r)
        both2, where2 = load(r2)
        m = jnp.max(top, axis=0, keepdims=True)
        tau = tau_ref[pl.ds(r, 1), :]
        c = tau * LOG2E
        top2 = None
        total = weighted = None
        nxt = 0
        for i in range(NBR):
            if i % 2 == 0:
                top2 = step1(1 - slot, both2, where2, nxt, top2); nxt += 1
            ex = jnp.exp2((s_buf[slot, i] - m) * c)
            s_buf[slot, i] = ex
            l8 = fold8(ex, jnp.sum)
            d8 = fold8(ex * dp_buf[slot, i], jnp.sum)
            total = l8 if total is None else total + l8
            weighted = d8 if weighted is None else weighted + d8
        norm = jnp.sum(total, axis=0, keepdims=True)
        inv = 1.0 / norm
        delta = jnp.sum(weighted, axis=0, keepdims=True) * inv
        dq = None
        for i in range(0, NBR, 2):
            us = []
            top2 = step1(1 - slot, both2, where2, nxt, top2); nxt += 1
            for j in (i, i + 1):
                p = s_buf[slot, j] * inv
                u = (p * (dp_buf[slot, j] - delta) * tau).astype(bf16)
                us.append(u)
                part = jnp.dot(jnp.concatenate([u, p.astype(bf16)], 1), both, preferred_element_type=f32)
                acc[where[j]] += part
            kt = jnp.concatenate([kt_tab[where[i]], kt_tab[where[i + 1]]], 1)
            d = jnp.dot(kt, jnp.concatenate(us, 0), preferred_element_type=f32)
            dq = d if dq is None else dq + d
        return dq, top2

    def pair(g, top):
        r = g * bpd
        dqs = []
        for rb in range(bpd):
            dq, top = advance(r + rb, rb % 2, top, jnp.minimum(r + rb + 1, nblk - 1))
            dqs.append(dq)
        turned = jnp.concatenate(dqs, 0).T.astype(bf16)
        dq_out[g ^ h] = turned
        return top

    both, where = load(0)
    top = None
    for i in range(NBR):
        top = step1(0, both, where, i, top)
    lax.fori_loop(0, n, pair, top)
    own_ref[...] = acc[pl.ds(0, nblk)]
    for k in range(1, parts):
        back[k - 1][...] = acc[pl.ds(nblk + (k - 1) * cap, cap)].astype(bf16)


def attend(idx, h, kv, qg, tau, borrowed, parts, cap, n, bpd):
    nblk = n * bpd
    slots = (parts - 1) * cap
    width = 2 * HD
    out = pl.pallas_call(
        functools.partial(attend_kernel, bool(qg), parts, cap, n, bpd),
        out_shape=[
            jax.ShapeDtypeStruct((n, BS, width), bf16),
            jax.ShapeDtypeStruct((nblk, BS, width), f32),
        ]
        + [jax.ShapeDtypeStruct((cap, BS, width), bf16)] * (parts - 1),
        in_specs=[SMEM, SMEM] + [VMEM] * (2 + len(qg) + len(borrowed)),
        out_specs=[VMEM] * (1 + parts),
        scratch_shapes=[
            pltpu.VMEM((nblk + slots, BS, width), bf16),
            pltpu.VMEM((nblk + slots, HD, BS), bf16),
            pltpu.VMEM((nblk + slots, BS, width), f32),
            pltpu.VMEM((bpd, NBR, BS, BS), f32),
            pltpu.VMEM((bpd, NBR, BS, BS), f32),
        ],
        compiler_params=params(),
        cost_estimate=cost(nblk * NBR * BS * BS * HD * 100, 6 << 20),
        name="attend",
    )(idx, h, kv, tau, *qg, *borrowed)
    return out[0], out[1], out[2:]


def collect_kernel(last, parts, cap, n, bpd, lists_ref, h_ref, own, *refs):
    returned, refs = refs[: parts - 1], refs[parts - 1 :]
    total = refs[-1]
    total[...] = own[...]
    for k in range(1, parts):
        for s in range(cap):
            total[lists_ref[k * cap + s]] += returned[k - 1][s].astype(f32)
    if not last:
        dq, out = refs[0], refs[1]
        out[:, pl.ds(0, BS)] = dq[...]
    for k in range(n):
        for b in range(bpd):
            block = total[k * bpd + b].astype(bf16)
            if last:
                refs[k][pl.ds(b * BS, BS)] = block
            else:
                out[k ^ h_ref[0], pl.ds((1 + b) * BS, BS)] = block


def collect(lists, h, own, returned, dq, parts, cap, n, bpd):
    last = dq is None
    if last:
        out = [jax.ShapeDtypeStruct((bpd * BS, 2 * HD), bf16)] * n
    else:
        out = [jax.ShapeDtypeStruct((n, (1 + bpd) * BS, 2 * HD), bf16)]
    more = [] if last else [dq]
    return pl.pallas_call(
        functools.partial(collect_kernel, last, parts, cap, n, bpd),
        out_shape=out,
        in_specs=[SMEM, SMEM] + [VMEM] * (parts + len(more)),
        out_specs=[VMEM] * len(out),
        scratch_shapes=[pltpu.VMEM(own.shape, f32)],
        compiler_params=params(),
        cost_estimate=cost(0, 4 << 20),
        name="collect",
    )(lists, h, own, *returned, *more)


def by_head(odd, one, two):
    low, high = jnp.where(odd, two, one), jnp.where(odd, one, two)
    return (
        jnp.concatenate([low[:, :HD], high[:, :HD]], 1),
        jnp.concatenate([low[:, HD:], high[:, HD:]], 1),
    )


def unpack_early_kernel(n, bpd, *refs):
    *arrived, last_q, gq, gk, gv = refs
    rows = bpd * BS
    never = jnp.zeros((rows, 2 * HD), jnp.int32) == 1
    never_q = jnp.zeros((BS, 2 * HD), jnp.int32) == 1
    top, tail = pl.ds(0, BS), pl.ds(BS, rows)
    for f, got in enumerate([*arrived, last_q]):
        for j in range(0, n, 2):
            cols = tile((f * n + j) // 2)
            for b, part in enumerate(by_head(never_q, got[j, top], got[j + 1, top])):
                gq[pl.ds(b * BS, BS), cols] = part
            if f < len(arrived):
                gk[:, cols], gv[:, cols] = by_head(never, got[j, tail], got[j + 1, tail])


def unpack_last_kernel(n, h_ref, *refs):
    last, gk, gv = refs[:n], refs[-2], refs[-1]
    h = h_ref[0]
    odd = jnp.broadcast_to(h & 1, last[0].shape) == 1
    for k in range(0, n, 2):
        cols = tile((h ^ k) >> 1)
        gk[:, cols], gv[:, cols] = by_head(odd, last[k][...], last[k + 1][...])


def unpack(arrived, last_q, total, h, phases, n, bpd):
    rows = bpd * BS
    shape = jax.ShapeDtypeStruct((rows, D), bf16)
    gq, gk, gv = pl.pallas_call(
        functools.partial(unpack_early_kernel, n, bpd),
        out_shape=[shape] * 3,
        in_specs=[VMEM] * (len(arrived) + 1),
        out_specs=[VMEM] * 3,
        compiler_params=params(),
        cost_estimate=cost(0, 8 << 20),
        name="unpack_early",
    )(*arrived, last_q)
    part = pl.BlockSpec((rows, n * HD), lambda i: (0, phases - 1))
    gk, gv = pl.pallas_call(
        functools.partial(unpack_last_kernel, n),
        grid=(1,),
        out_shape=[shape] * 2,
        in_specs=[SMEM] + [VMEM] * n + [ANY] * 2,
        out_specs=[part] * 2,
        input_output_aliases={n + 1: 0, n + 2: 1},
        compiler_params=params(),
        cost_estimate=cost(0, 2 << 20),
        name="unpack_last",
    )(h, *total, gk, gv)
    return gq, gk, gv


def swap(x, k, axis, size):
    return lax.ppermute(x, axis, [(i, i ^ k) for i in range(size)])


def body(node_queries, node_keys, node_values, out_grad, degrees, neighbor_blocks, send_slots):
    n = lax.axis_size("head")
    parts = lax.axis_size("dom")
    cap = send_slots.shape[2]
    phases = H // n
    rows = node_queries.shape[0]
    bpd = rows // BS
    nblk = n * bpd
    me = lax.axis_index("dom")
    head = lax.axis_index("head")
    h = head.astype(jnp.int32).reshape(1)
    hop = jnp.arange(parts, dtype=jnp.int32)
    pick = (hop[:, None] == (hop[None, :] ^ me)).astype(jnp.int32)
    step = jnp.arange(n, dtype=jnp.int32)
    turn = (step[:, None] == (step[None, :] ^ head)).astype(jnp.int32)

    def local(b):
        return ((b // bpd) ^ head) * bpd + b % bpd

    def turned(x):
        y = x.reshape(n, -1)
        return jnp.sum(turn[:, :, None] * y[None], axis=1).reshape(x.shape)

    mine = jnp.maximum(lax.dynamic_index_in_dim(send_slots, me, 0, keepdims=False), 0)
    lists = local(jnp.sum(pick[:, :, None] * mine[None], axis=1).reshape(-1))
    away = neighbor_blocks - nblk
    moved = nblk + ((away // cap) ^ me) * cap + away % cap - cap
    idx = turned(jnp.where(away < 0, local(neighbor_blocks), moved)).reshape(-1)
    count = turned(degrees.reshape(nblk, BS))
    tau = jnp.log(count.astype(f32)) / math.log(64.0) / math.sqrt(HD)

    def spread(x):
        return lax.all_to_all(x, "head", split_axis=0, concat_axis=0, tiled=True)

    def trade(x):
        return [x[0]] + [swap(x[k], k, "head", n) for k in range(1, n)]

    kv = [x.reshape(bpd, BS, 2 * HD) for x in trade(pieces(node_keys, node_values, n, h))]
    early = 1 + n // 4
    first, kv[1:early] = lax.optimization_barrier((pack_one(node_queries, out_grad, n), kv[1:early]))
    qg = [spread(first).reshape(n, bpd, BS, 2 * HD)]
    later = []
    for f in range(1, phases):
        sent, qg = lax.optimization_barrier((pack(node_queries, node_keys, node_values, out_grad, f, n), qg))
        later.append(spread(sent).reshape(n, 2 * bpd, BS, 2 * HD))
    arrived, total, sent = [], [], None
    for f in range(phases):
        last = f + 1 == phases
        if f:
            kv, qg = [later[f - 1]], []
        lent = lend(lists, h, kv, parts, cap, bpd)
        borrowed = [swap(x, k + 1, "dom", parts) for k, x in enumerate(lent[-(parts - 1) :])]
        if f:
            borrowed, _ = lax.optimization_barrier((borrowed, sent))
            arrived.append(spread(sent))
        dq, own, back = attend(idx, h, lent[0] if f == 0 else kv[0], qg, tau, borrowed, parts, cap, n, bpd)
        returned = [swap(back[k - 1], k, "dom", parts) for k in range(1, parts)]
        if f:
            dq, arrived[-1], returned = lax.optimization_barrier((dq, arrived[-1], returned))
        if last:
            dq_all = spread(dq)
        out = collect(lists, h, own, returned, None if last else dq, parts, cap, n, bpd)
        if last:
            total = trade(out)
        else:
            sent = out[0]
    return tuple(unpack(arrived, dq_all, total, h, phases, n, bpd))


def solution(mesh):
    placed = (
        P(("dom", "head"), None),
        P(("dom", "head"), None),
        P(("dom", "head"), None),
        P(("dom", "head"), None),
        P("dom"),
        P("dom", None),
        P(),
    )
    return jax.shard_map(
        body,
        mesh=mesh,
        in_specs=placed,
        out_specs=(P(("dom", "head"), None), P(("dom", "head"), None), P(("dom", "head"), None)),
        check_vma=False,
    )
```

```python
import functools
import math

import jax
import jax.numpy as jnp
from jax import lax
from jax.experimental import pallas as pl
from jax.experimental.pallas import tpu as pltpu
from jax.sharding import PartitionSpec as P

D = 1024
H = 16
NBR = 12
BS = 128
HD = D // H
LOG2E = 1.4426950408889634
VMEM_LIMIT = 56 << 20

bf16 = jnp.bfloat16
f32 = jnp.float32


def params():
    return pltpu.CompilerParams(vmem_limit_bytes=VMEM_LIMIT)


def cost(flops, bytes_accessed):
    return pl.CostEstimate(flops=flops, bytes_accessed=bytes_accessed, transcendentals=0)


VMEM = pl.BlockSpec(memory_space=pltpu.VMEM)
SMEM = pl.BlockSpec(memory_space=pltpu.SMEM)
ANY = pl.BlockSpec(memory_space=pl.ANY)


def pack_kernel(first, n, q_ref, k_ref, v_ref, g_ref, out_ref):
    rows = q_ref.shape[0]
    for i in range(0, n, 2):
        cols = tile((first * n + i) // 2)
        for at, (x, y) in ((0, (k_ref[:, cols], v_ref[:, cols])), (rows, (q_ref[:, cols], g_ref[:, cols]))):
            out_ref[i, pl.ds(at, rows)] = jnp.concatenate([x[:, :HD], y[:, :HD]], 1)
            out_ref[i + 1, pl.ds(at, rows)] = jnp.concatenate([x[:, HD:], y[:, HD:]], 1)


def pack(queries, keys, values, grads, first, n):
    rows = queries.shape[0]
    return pl.pallas_call(
        functools.partial(pack_kernel, first, n),
        out_shape=jax.ShapeDtypeStruct((n, 2 * rows, 2 * HD), bf16),
        in_specs=[VMEM] * 4,
        out_specs=VMEM,
        compiler_params=params(),
        cost_estimate=cost(0, 8 * rows * D),
        name="pack",
    )(queries, keys, values, grads)


def tile(at):
    return pl.ds(pl.multiple_of(at * 2 * HD, 2 * HD), 2 * HD)


def pack_one_kernel(n, x_ref, y_ref, out_ref):
    for i in range(0, n, 2):
        cols = tile(i // 2)
        x, y = x_ref[:, cols], y_ref[:, cols]
        out_ref[i] = jnp.concatenate([x[:, :HD], y[:, :HD]], 1)
        out_ref[i + 1] = jnp.concatenate([x[:, HD:], y[:, HD:]], 1)


def pack_one(x, y, n):
    rows = x.shape[0]
    return pl.pallas_call(
        functools.partial(pack_one_kernel, n),
        out_shape=jax.ShapeDtypeStruct((n, rows, 2 * HD), bf16),
        in_specs=[VMEM] * 2,
        out_specs=VMEM,
        compiler_params=params(),
        cost_estimate=cost(0, 8 * rows * D),
        name="pack_one",
    )(x, y)


def pieces_kernel(n, h_ref, x_ref, y_ref, *outs):
    rows = x_ref.shape[0]
    h = h_ref[0]
    odd = jnp.broadcast_to(h & 1, (rows, 2 * HD)) == 1
    for k in range(0, n, 2):
        cols = tile((h ^ k) >> 1)
        x, y = x_ref[:, cols], y_ref[:, cols]
        even_head = jnp.concatenate([x[:, :HD], y[:, :HD]], 1)
        odd_head = jnp.concatenate([x[:, HD:], y[:, HD:]], 1)
        outs[k][...] = jnp.where(odd, odd_head, even_head)
        outs[k + 1][...] = jnp.where(odd, even_head, odd_head)


def pieces(x, y, n, h):
    rows = x.shape[0]
    return pl.pallas_call(
        functools.partial(pieces_kernel, n),
        out_shape=[jax.ShapeDtypeStruct((rows, 2 * HD), bf16)] * n,
        in_specs=[SMEM] + [VMEM] * 2,
        out_specs=[VMEM] * n,
        compiler_params=params(),
        cost_estimate=cost(0, 8 * rows * D),
        name="pieces",
    )(h, x, y)


def lend_kernel(parts, cap, bpd, lists_ref, h_ref, *refs):
    outs = refs[-(parts - 1) :]
    kvs = refs[: -(parts - 1)]
    h = h_ref[0]
    if len(kvs) > 1:
        source, h = kvs[-1], 0
        for k, piece in enumerate(kvs[:-1]):
            source[k] = piece[...]
    else:
        source = kvs[0]
    for k in range(1, parts):
        for s in range(cap):
            b = lists_ref[k * cap + s]
            outs[k - 1][s] = source[lax.div(b, bpd) ^ h, lax.rem(b, bpd)]


def lend(lists, h, kv, parts, cap, bpd):
    whole = [] if len(kv) == 1 else [jax.ShapeDtypeStruct((len(kv), bpd, BS, 2 * HD), bf16)]
    return pl.pallas_call(
        functools.partial(lend_kernel, parts, cap, bpd),
        out_shape=whole + [jax.ShapeDtypeStruct((cap, BS, 2 * HD), bf16)] * (parts - 1),
        in_specs=[SMEM, SMEM] + [VMEM] * len(kv),
        out_specs=[VMEM] * (len(whole) + parts - 1),
        compiler_params=params(),
        cost_estimate=cost(0, 4 * parts * cap * BS * 4 * HD),
        name="lend",
    )(lists, h, *kv)


def attend_kernel(paired, parts, cap, n, bpd, idx_ref, h_ref, kv_ref, tau_ref, *refs):
    qg, refs = (refs[0], refs[1:]) if paired else (None, refs)
    h = h_ref[0]
    borrowed, refs = refs[: parts - 1], refs[parts - 1 :]
    dq_out, own_ref, refs = refs[0], refs[1], refs[2:]
    back = refs[: parts - 1]
    tab, kt_tab, acc, s_buf, dp_buf = refs[parts - 1 :]
    nblk = n * bpd
    slots = (parts - 1) * cap

    def enter(t, block):
        tab[t] = block
        kt_tab[t] = block.astype(f32).T[:HD].astype(bf16)

    acc[...] = jnp.zeros_like(acc)
    for k in range(n):
        for b in range(bpd):
            enter(k * bpd + b, kv_ref[k if paired else k ^ h, b])
    for k in range(1, parts):
        for b in range(cap):
            enter(nblk + (k - 1) * cap + b, borrowed[k - 1][b])
    lane = lax.broadcasted_iota(jnp.int32, (BS, 2 * HD), 1)
    low = lane < HD
    zero = jnp.zeros((BS, 2 * HD), bf16)

    def fold8(x, op):
        return op(x.reshape(BS // 8, 8, BS), axis=0)

    def load(r):
        at, row = lax.div(r, bpd) ^ h, lax.rem(r, bpd)
        block = qg[at, row] if paired else kv_ref[at, bpd + row]
        both = jnp.concatenate([jnp.where(low, block, zero), jnp.where(low, zero, block)], 0)
        return both, [idx_ref[r * NBR + i] for i in range(NBR)]

    def step1(slot, both, where, i, top):
        rr = lax.dot_general(tab[where[i]], both, (((1,), (1,)), ((), ())), preferred_element_type=f32)
        s = rr[:, :BS]
        s_buf[slot, i] = s
        dp_buf[slot, i] = rr[:, BS:]
        m8 = fold8(s, jnp.max)
        return m8 if top is None else jnp.maximum(top, m8)

    def advance(r, slot, top, r2):
        both, where = load(r)
        both2, where2 = load(r2)
        m = jnp.max(top, axis=0, keepdims=True)
        tau = tau_ref[pl.ds(r, 1), :]
        c = tau * LOG2E
        top2 = None
        total = weighted = None
        nxt = 0
        for i in range(NBR):
            if i % 4 < 3:
                top2 = step1(1 - slot, both2, where2, nxt, top2)
                nxt += 1
            ex = jnp.exp2((s_buf[slot, i] - m) * c)
            s_buf[slot, i] = ex
            l8 = fold8(ex, jnp.sum)
            d8 = fold8(ex * dp_buf[slot, i], jnp.sum)
            total = l8 if total is None else total + l8
            weighted = d8 if weighted is None else weighted + d8
        norm = jnp.sum(total, axis=0, keepdims=True)
        inv = 1.0 / norm
        delta = jnp.sum(weighted, axis=0, keepdims=True) * inv
        dq = None
        for i in range(0, NBR, 2):
            us = []
            if nxt < NBR:
                top2 = step1(1 - slot, both2, where2, nxt, top2)
                nxt += 1
            for j in (i, i + 1):
                p = s_buf[slot, j] * inv
                u = (p * (dp_buf[slot, j] - delta) * tau).astype(bf16)
                us.append(u)
                part = jnp.dot(jnp.concatenate([u, p.astype(bf16)], 1), both, preferred_element_type=f32)
                acc[where[j]] += part
            kt = jnp.concatenate([kt_tab[where[i]], kt_tab[where[i + 1]]], 1)
            d = jnp.dot(kt, jnp.concatenate(us, 0), preferred_element_type=f32)
            dq = d if dq is None else dq + d
        return dq, top2

    def pair(g, top):
        r = g * bpd
        dqs = []
        for rb in range(bpd):
            dq, top = advance(r + rb, rb % 2, top, jnp.minimum(r + rb + 1, nblk - 1))
            dqs.append(dq)
        turned = jnp.concatenate(dqs, 0).T.astype(bf16)
        dq_out[g ^ h] = turned
        return top

    both, where = load(0)
    top = None
    for i in range(NBR):
        top = step1(0, both, where, i, top)
    lax.fori_loop(0, n, pair, top)
    own_ref[...] = acc[pl.ds(0, nblk)]
    for k in range(1, parts):
        back[k - 1][...] = acc[pl.ds(nblk + (k - 1) * cap, cap)].astype(bf16)


def attend(idx, h, kv, qg, tau, borrowed, parts, cap, n, bpd):
    nblk = n * bpd
    slots = (parts - 1) * cap
    width = 2 * HD
    out = pl.pallas_call(
        functools.partial(attend_kernel, bool(qg), parts, cap, n, bpd),
        out_shape=[
            jax.ShapeDtypeStruct((n, BS, width), bf16),
            jax.ShapeDtypeStruct((nblk, BS, width), f32),
        ]
        + [jax.ShapeDtypeStruct((cap, BS, width), bf16)] * (parts - 1),
        in_specs=[SMEM, SMEM] + [VMEM] * (2 + len(qg) + len(borrowed)),
        out_specs=[VMEM] * (1 + parts),
        scratch_shapes=[
            pltpu.VMEM((nblk + slots, BS, width), bf16),
            pltpu.VMEM((nblk + slots, HD, BS), bf16),
            pltpu.VMEM((nblk + slots, BS, width), f32),
            pltpu.VMEM((bpd, NBR, BS, BS), f32),
            pltpu.VMEM((bpd, NBR, BS, BS), f32),
        ],
        compiler_params=params(),
        cost_estimate=cost(nblk * NBR * BS * BS * HD * 100, 6 << 20),
        name="attend",
    )(idx, h, kv, tau, *qg, *borrowed)
    return out[0], out[1], out[2:]


def collect_kernel(last, parts, cap, n, bpd, lists_ref, h_ref, own, *refs):
    returned, refs = refs[: parts - 1], refs[parts - 1 :]
    total = refs[-1]
    total[...] = own[...]
    for k in range(1, parts):
        for s in range(cap):
            total[lists_ref[k * cap + s]] += returned[k - 1][s].astype(f32)
    if not last:
        dq, out = refs[0], refs[1]
        out[:, pl.ds(0, BS)] = dq[...]
    for k in range(n):
        for b in range(bpd):
            block = total[k * bpd + b].astype(bf16)
            if last:
                refs[k][pl.ds(b * BS, BS)] = block
            else:
                out[k ^ h_ref[0], pl.ds((1 + b) * BS, BS)] = block


def collect(lists, h, own, returned, dq, parts, cap, n, bpd):
    last = dq is None
    if last:
        out = [jax.ShapeDtypeStruct((bpd * BS, 2 * HD), bf16)] * n
    else:
        out = [jax.ShapeDtypeStruct((n, (1 + bpd) * BS, 2 * HD), bf16)]
    more = [] if last else [dq]
    return pl.pallas_call(
        functools.partial(collect_kernel, last, parts, cap, n, bpd),
        out_shape=out,
        in_specs=[SMEM, SMEM] + [VMEM] * (parts + len(more)),
        out_specs=[VMEM] * len(out),
        scratch_shapes=[pltpu.VMEM(own.shape, f32)],
        compiler_params=params(),
        cost_estimate=cost(0, 4 << 20),
        name="collect",
    )(lists, h, own, *returned, *more)


def by_head(odd, one, two):
    low, high = jnp.where(odd, two, one), jnp.where(odd, one, two)
    return (
        jnp.concatenate([low[:, :HD], high[:, :HD]], 1),
        jnp.concatenate([low[:, HD:], high[:, HD:]], 1),
    )


def unpack_early_kernel(n, bpd, *refs):
    *arrived, last_q, gq, gk, gv = refs
    rows = bpd * BS
    never = jnp.zeros((rows, 2 * HD), jnp.int32) == 1
    never_q = jnp.zeros((BS, 2 * HD), jnp.int32) == 1
    top, tail = pl.ds(0, BS), pl.ds(BS, rows)
    for f, got in enumerate([*arrived, last_q]):
        for j in range(0, n, 2):
            cols = tile((f * n + j) // 2)
            for b, part in enumerate(by_head(never_q, got[j, top], got[j + 1, top])):
                gq[pl.ds(b * BS, BS), cols] = part
            if f < len(arrived):
                gk[:, cols], gv[:, cols] = by_head(never, got[j, tail], got[j + 1, tail])


def unpack_last_kernel(n, h_ref, *refs):
    last, gk, gv = refs[:n], refs[-2], refs[-1]
    h = h_ref[0]
    odd = jnp.broadcast_to(h & 1, last[0].shape) == 1
    for k in range(0, n, 2):
        cols = tile((h ^ k) >> 1)
        gk[:, cols], gv[:, cols] = by_head(odd, last[k][...], last[k + 1][...])


def unpack(arrived, last_q, total, h, phases, n, bpd):
    rows = bpd * BS
    shape = jax.ShapeDtypeStruct((rows, D), bf16)
    gq, gk, gv = pl.pallas_call(
        functools.partial(unpack_early_kernel, n, bpd),
        out_shape=[shape] * 3,
        in_specs=[VMEM] * (len(arrived) + 1),
        out_specs=[VMEM] * 3,
        compiler_params=params(),
        cost_estimate=cost(0, 8 << 20),
        name="unpack_early",
    )(*arrived, last_q)
    part = pl.BlockSpec((rows, n * HD), lambda i: (0, phases - 1))
    gk, gv = pl.pallas_call(
        functools.partial(unpack_last_kernel, n),
        grid=(1,),
        out_shape=[shape] * 2,
        in_specs=[SMEM] + [VMEM] * n + [ANY] * 2,
        out_specs=[part] * 2,
        input_output_aliases={n + 1: 0, n + 2: 1},
        compiler_params=params(),
        cost_estimate=cost(0, 2 << 20),
        name="unpack_last",
    )(h, *total, gk, gv)
    return gq, gk, gv


def swap(x, k, axis, size):
    return lax.ppermute(x, axis, [(i, i ^ k) for i in range(size)])


def body(node_queries, node_keys, node_values, out_grad, degrees, neighbor_blocks, send_slots):
    n = lax.axis_size("head")
    parts = lax.axis_size("dom")
    cap = send_slots.shape[2]
    phases = H // n
    rows = node_queries.shape[0]
    bpd = rows // BS
    nblk = n * bpd
    me = lax.axis_index("dom")
    head = lax.axis_index("head")
    h = head.astype(jnp.int32).reshape(1)
    hop = jnp.arange(parts, dtype=jnp.int32)
    pick = (hop[:, None] == (hop[None, :] ^ me)).astype(jnp.int32)
    step = jnp.arange(n, dtype=jnp.int32)
    turn = (step[:, None] == (step[None, :] ^ head)).astype(jnp.int32)

    def local(b):
        return ((b // bpd) ^ head) * bpd + b % bpd

    def turned(x):
        y = x.reshape(n, -1)
        return jnp.sum(turn[:, :, None] * y[None], axis=1).reshape(x.shape)

    mine = jnp.maximum(lax.dynamic_index_in_dim(send_slots, me, 0, keepdims=False), 0)
    lists = local(jnp.sum(pick[:, :, None] * mine[None], axis=1).reshape(-1))
    away = neighbor_blocks - nblk
    moved = nblk + ((away // cap) ^ me) * cap + away % cap - cap
    idx = turned(jnp.where(away < 0, local(neighbor_blocks), moved)).reshape(-1)
    count = turned(degrees.reshape(nblk, BS))
    tau = jnp.log(count.astype(f32)) / math.log(64.0) / math.sqrt(HD)

    def spread(x):
        return lax.all_to_all(x, "head", split_axis=0, concat_axis=0, tiled=True)

    def trade(x):
        return [x[0]] + [swap(x[k], k, "head", n) for k in range(1, n)]

    kv = [x.reshape(bpd, BS, 2 * HD) for x in trade(pieces(node_keys, node_values, n, h))]
    early = 1 + n // 4
    first, kv[1:early] = lax.optimization_barrier((pack_one(node_queries, out_grad, n), kv[1:early]))
    qg = [spread(first).reshape(n, bpd, BS, 2 * HD)]
    later = []
    for f in range(1, phases):
        sent, qg = lax.optimization_barrier((pack(node_queries, node_keys, node_values, out_grad, f, n), qg))
        later.append(spread(sent).reshape(n, 2 * bpd, BS, 2 * HD))
    arrived, total, sent = [], [], None
    for f in range(phases):
        last = f + 1 == phases
        if f:
            kv, qg = [later[f - 1]], []
        lent = lend(lists, h, kv, parts, cap, bpd)
        borrowed = [swap(x, k + 1, "dom", parts) for k, x in enumerate(lent[-(parts - 1) :])]
        if f:
            borrowed, _ = lax.optimization_barrier((borrowed, sent))
            arrived.append(spread(sent))
        dq, own, back = attend(idx, h, lent[0] if f == 0 else kv[0], qg, tau, borrowed, parts, cap, n, bpd)
        returned = [swap(back[k - 1], k, "dom", parts) for k in range(1, parts)]
        if f:
            dq, arrived[-1], returned = lax.optimization_barrier((dq, arrived[-1], returned))
        if last:
            dq_all = spread(dq)
        out = collect(lists, h, own, returned, None if last else dq, parts, cap, n, bpd)
        if last:
            total = trade(out)
        else:
            sent = out[0]
    return tuple(unpack(arrived, dq_all, total, h, phases, n, bpd))


def solution(mesh):
    placed = (
        P(("dom", "head"), None),
        P(("dom", "head"), None),
        P(("dom", "head"), None),
        P(("dom", "head"), None),
        P("dom"),
        P("dom", None),
        P(),
    )
    return jax.shard_map(
        body,
        mesh=mesh,
        in_specs=placed,
        out_specs=(P(("dom", "head"), None), P(("dom", "head"), None), P(("dom", "head"), None)),
        check_vma=False,
    )
```
